32 devices in a mesh: gz: 4 (over y, core), xy: 8 (over z, x).
Axes of the slice: x: 2, y: 2, z: 4, core: 2. Of those that a mesh axis runs over, the one named last changes fastest.
Arguments:
- volume: bfloat16 [32, 64, 2048], P('gz', 'xy'), may hold values from -6 to 6
- backbone_weight: bfloat16 [64, 1728], replicated, may hold values from -0.15625 to 0.15625
- refine_weight: bfloat16 [64, 1728], replicated, may hold values from -0.15625 to 0.15625
- mix_weight: bfloat16 [64, 64], replicated, may hold values from -0.75 to 0.75
- tile_cot: bfloat16 [4, 8, 8, 2, 8, 8, 512], P('gz', 'xy'), may hold values from -6 to 6
- tile_slot: int32 [4, 8, 8, 2], P('gz', 'xy'), may hold values from 0 to 3
- tile_count: int32 [4, 8, 8], P('gz'), may hold values from 0 to 2, as said below
Outputs:
- volume_grad: bfloat16 [32, 64, 2048], P('gz', 'xy')
- backbone_step: float32 [64, 1728], replicated
- refine_step: float32 [64, 1728], replicated
- mix_step: float32 [64, 64], replicated
The draws below stay inside these ranges and needn't reach their ends.
Inputs may be any that keep to these rules, and one draw needn't show every extreme that they name: `tile_count`: in every slab each owner receives exactly 8 live slots in all; some pairs of brick and owner use all 2 slots. `tile_slot`: only slots j < tile_count[g, s, d] are read.
All inputs are finite; a program needn't handle non-finite values.
Results may differ from the reference program's by a relative error of at most 0.0059.
Values may be sent and summed in bfloat16 or wider, within the bound.
A program may use at most 192 MiB of HBM per device.

```python
import jax
import jax.numpy as jnp
from jax import lax

C = 64
TE = 8
CAP = 2
BZ = 8
BY = 8
NX = 32
NZ = 32
NY = 64
TPB = 4
OWN = 8
N_GZ = 4
N_XY = 8


def draw_tile_count(key, part):
    heavy_count = N_XY // 8
    light_count = N_XY - heavy_count

    def one_slab(slab_key):
        order_key, shift_key = jax.random.split(slab_key)
        source_rank = jax.random.permutation(order_key, N_XY).astype(jnp.int32)
        shifts = jax.random.randint(shift_key, (N_XY,), 0, light_count).astype(jnp.int32)
        light_rank = jnp.clip(source_rank - heavy_count, 0, light_count - 1)
        pattern = jnp.where((light_rank[:, None] + shifts[None, :]) % light_count % 3 == 0, CAP, 0)
        return jnp.where(source_rank[:, None] < heavy_count, CAP, pattern).astype(jnp.int32)
    return jax.vmap(one_slab)(jax.random.split(key, N_GZ))


def plant(values, key, smallest, high):
    longest = values.shape.index(max(values.shape))
    spots = []
    for shift in (0, 1):
        where = [jax.random.randint(jax.random.fold_in(key, axis), (), 0, length) for axis, length in enumerate(values.shape)]
        where[longest] = (where[longest] + shift) % values.shape[longest]
        spots.append(tuple(where))
    return values.at[spots[0]].set(smallest).at[spots[1]].set(high)


def steps_of(key, shape, pieces, low, top_value):
    def one(dim, shards_of):
        heights = jax.random.uniform(jax.random.fold_in(jax.random.fold_in(key, 6), dim), (shards_of,), jnp.float32, low / len(pieces), top_value / len(pieces))
        return jnp.repeat(jnp.exp(heights), shape[dim] // shards_of).reshape((-1,) + (1,) * (len(shape) - dim - 1))

    factor_of = one(*pieces[0])
    for cut in pieces[1:]:
        factor_of = factor_of * one(*cut)
    return factor_of


def centred(own_key, dims, scale, most, shards=(), held_as=jnp.bfloat16):
    factor_of = steps_of(own_key, dims, shards, -0.22, 0.18) if shards else 1.0
    array = jax.random.normal(own_key, dims, jnp.float32) * scale * factor_of
    return jnp.minimum(jnp.maximum(array, -most), most).astype(held_as)


def setup_inputs(seed: int = 0) -> dict:
    arg_keys = jax.random.split(jax.random.key(seed), 8)
    return {
        "volume": centred(arg_keys[0], (NZ, NY, NX * C), 1.0, 6.0, ((0, 4), (1, 8))),
        "backbone_weight": centred(arg_keys[1], (C, 27 * C), (27 * C) ** -0.5, 0.15625),
        "refine_weight": centred(arg_keys[2], (C, 27 * C), (27 * C) ** -0.5, 0.15625),
        "mix_weight": centred(arg_keys[3], (C, C), C ** -0.5, 0.75),
        "tile_cot": centred(arg_keys[4], (N_GZ, N_XY, N_XY, CAP, TE, TE, TE * C), 1.0, 6.0, ((0, 4), (1, 8))),
        "tile_slot": plant(jax.random.randint(arg_keys[5], (N_GZ, N_XY, N_XY, CAP), 0, TPB), jax.random.fold_in(arg_keys[5], 1), 0, TPB - 1).astype(jnp.int32),
        "tile_count": draw_tile_count(jax.random.fold_in(arg_keys[7], 71), 0),
    }


EPSILON = 1e-06

def offset_list():
    return [(step_z, step_y, step_x) for step_z in range(3) for step_y in range(3) for step_x in range(3)]

def narrowed(values):
    return lax.optimization_barrier(values.astype(jnp.bfloat16)).astype(jnp.float32)

def pad_cells(values):
    widths = [(0, 0)] * (values.ndim - 4) + [(1, 1), (1, 1), (1, 1), (0, 0)]
    return jnp.pad(values, widths)

def window_at(padded, corner, extent):
    return padded[..., corner[0]:corner[0] + extent[0], corner[1]:corner[1] + extent[1], corner[2]:corner[2] + extent[2], :]

def conv_apply(padded, weight, extent):
    channels = padded.shape[-1]
    result = None
    for offset_id, corner in enumerate(offset_list()):
        kernel = weight[:, offset_id * channels:(offset_id + 1) * channels]
        summand = jnp.einsum('...i,io->...o', window_at(padded, corner, extent), kernel)
        result = summand if result is None else result + summand
    return result

def conv_transpose(padded_grad, weight, extent):
    channels = padded_grad.shape[-1]
    result = None
    for offset_id, corner in enumerate(offset_list()):
        kernel = weight[:, offset_id * channels:(offset_id + 1) * channels]
        mirror = (2 - corner[0], 2 - corner[1], 2 - corner[2])
        summand = jnp.einsum('...o,io->...i', window_at(padded_grad, mirror, extent), kernel)
        result = summand if result is None else result + summand
    return result

def conv_weight_grad(padded, grad, extent):
    channels = padded.shape[-1]
    flat_grad = grad.reshape(-1, channels)
    blocks = []
    for corner in offset_list():
        window = window_at(padded, corner, extent).reshape(-1, channels)
        blocks.append(jnp.dot(window.T, flat_grad, precision=lax.Precision.HIGHEST))
    return jnp.concatenate(blocks, axis=1)

def normalized(gradient):
    return gradient / jnp.sqrt(jnp.mean(gradient * gradient) + EPSILON)

def refine_tiles(tiles, cots, refine_weight, mix_weight):
    batch_size = tiles.shape[0]
    tile_edge = tiles.shape[1]
    channels = mix_weight.shape[0]
    extent = (tile_edge, tile_edge, tile_edge)
    shaped = tiles.reshape(batch_size, tile_edge, tile_edge, tile_edge, channels).astype(jnp.float32)
    upstream = cots.reshape(batch_size, tile_edge, tile_edge, tile_edge, channels).astype(jnp.float32)
    weight_one = refine_weight.astype(jnp.float32)
    weight_two = mix_weight.astype(jnp.float32)
    padded = pad_cells(shaped)
    before = conv_apply(padded, weight_one, extent)
    gated_act = narrowed(jax.nn.silu(before))
    mix_part = jnp.dot(gated_act.reshape(-1, channels).T, upstream.reshape(-1, channels), precision=lax.Precision.HIGHEST)
    gated_grad = jnp.einsum('...o,io->...i', upstream, weight_two)
    sigmoid_of = jax.nn.sigmoid(before)
    before_grad = narrowed(gated_grad * sigmoid_of * (1.0 + before * (1.0 - sigmoid_of)))
    refine_part = conv_weight_grad(padded, before_grad, extent)
    tile_grad = upstream + conv_transpose(pad_cells(before_grad), weight_one, extent)
    return (tile_grad.astype(jnp.bfloat16).reshape(tiles.shape), refine_part, mix_part)

def reference(volume, backbone_weight, refine_weight, mix_weight, tile_cot, tile_slot, tile_count):
    field = volume.astype(jnp.float32).reshape(NZ, NY, NX, C)
    padded_in = pad_cells(field)
    weight_back = backbone_weight.astype(jnp.float32)
    feature = (field + conv_apply(padded_in, weight_back, (NZ, NY, NX))).astype(jnp.bfloat16)
    blocked = feature.reshape(N_GZ, BZ // TE, TE, N_XY, BY // TE, TE, NX // TE, TE, C)
    all_tiles = blocked.transpose(0, 3, 1, 4, 6, 2, 5, 7, 8).reshape(N_GZ, N_XY * TPB, TE, TE, TE * C)
    slot_total = N_XY * CAP
    lanes_cap = jnp.arange(CAP, dtype=jnp.int32)

    def per_owner(pair_id):
        slab_id = pair_id // N_XY
        owner_id = pair_id % N_XY
        counts_in = jnp.take(tile_count[slab_id], owner_id, axis=1)
        slots_in = jnp.take(tile_slot[slab_id], owner_id, axis=1)
        cots_in = jnp.take(tile_cot[slab_id], owner_id, axis=1).reshape(slot_total, TE, TE, TE * C)
        valid_slot = (lanes_cap[None, :] < counts_in[:, None]).reshape(slot_total)
        slot_rank = jnp.cumsum(valid_slot.astype(jnp.int32)) - 1
        chooser = (slot_rank[None, :] == jnp.arange(OWN, dtype=jnp.int32)[:, None]) & valid_slot[None, :]
        source_rows = (jnp.arange(N_XY, dtype=jnp.int32)[:, None] * TPB + slots_in).reshape(slot_total)
        tile_rows = lax.optimization_barrier(jnp.sum(jnp.where(chooser, source_rows[None, :], 0), axis=1)).astype(jnp.int32)
        slot_rows = lax.optimization_barrier(jnp.sum(jnp.where(chooser, jnp.arange(slot_total, dtype=jnp.int32)[None, :], 0), axis=1)).astype(jnp.int32)
        chosen = jnp.take(all_tiles[slab_id], tile_rows, axis=0)
        chosen_cot = jnp.take(cots_in, slot_rows, axis=0)
        tile_grad, refine_part, mix_part = refine_tiles(chosen, chosen_cot, refine_weight, mix_weight)
        return (tile_grad, refine_part, mix_part, (slab_id * (N_XY * TPB) + tile_rows).astype(jnp.int32))
    tile_grads, refine_parts, mix_parts, segment_ids = lax.map(per_owner, jnp.arange(N_GZ * N_XY, dtype=jnp.int32))
    summed = jax.ops.segment_sum(tile_grads.astype(jnp.float32).reshape(N_GZ * N_XY * OWN, TE * TE * TE * C), segment_ids.reshape(-1), num_segments=N_GZ * N_XY * TPB)
    placed = summed.reshape(N_GZ, N_XY, BZ // TE, BY // TE, NX // TE, TE, TE, TE, C).transpose(0, 2, 5, 1, 3, 6, 4, 7, 8)
    feature_grad = narrowed(placed.reshape(NZ, NY, NX, C))
    volume_grad = (feature_grad + conv_transpose(pad_cells(feature_grad), weight_back, (NZ, NY, NX))).astype(jnp.bfloat16).reshape(NZ, NY, NX * C)
    backbone_sum = conv_weight_grad(padded_in, feature_grad, (NZ, NY, NX))
    return (volume_grad, normalized(backbone_sum), normalized(lax.optimization_barrier(jnp.sum(refine_parts, axis=0))), normalized(lax.optimization_barrier(jnp.sum(mix_parts, axis=0))))
```

```python
import functools

import jax
import jax.numpy as jnp
from jax import lax
from jax.experimental import pallas as pl
from jax.experimental.pallas import tpu as pltpu
from jax.sharding import PartitionSpec as P

EPSILON = 1e-06
F32 = jnp.float32
BF16 = jnp.bfloat16
VMEM = pl.BlockSpec(memory_space=pltpu.VMEM)
ANY = pl.BlockSpec(memory_space=pl.ANY)
MESH = pl.DeviceIdType.MESH


def neighbours():
    return [(dz, dy) for dz in (-1, 0, 1) for dy in (-1, 0, 1) if (dz, dy) != (0, 0)]


def near(step, size):
    if step == 0:
        return pl.ds(1, size)
    return pl.ds(size, 1) if step > 0 else pl.ds(1, 1)


def far(step, size):
    if step == 0:
        return pl.ds(1, size)
    return pl.ds(0, 1) if step > 0 else pl.ds(size + 1, 1)


class Rims:
    def __init__(self, sizes, place, framed, depth, rows, lanes, send, recv):
        self.sizes, self.place, self.framed = sizes, place, framed
        self.depth, self.rows, self.lanes = depth, rows, lanes
        self.send, self.recv = send, recv

    def there(self, dz, dy):
        (n_gz, n_xy), (gz, xy) = self.sizes, self.place
        inside = (gz + dz >= 0) & (gz + dz < n_gz) & (xy + dy >= 0) & (xy + dy < n_xy)
        return inside, (gz + dz, xy + dy)

    def copy(self, dz, dy, number):
        cells = (slice(None), pl.ds(0, self.lanes))
        return pltpu.make_async_remote_copy(
            src_ref=self.framed.at[(near(dz, self.depth), near(dy, self.rows)) + cells],
            dst_ref=self.framed.at[(far(dz, self.depth), far(dy, self.rows)) + cells],
            send_sem=self.send.at[number],
            recv_sem=self.recv.at[number],
            device_id=self.there(dz, dy)[1],
            device_id_type=MESH,
        )

    def start(self):
        for number, (dz, dy) in enumerate(neighbours()):

            @pl.when(self.there(dz, dy)[0])
            def _():
                self.copy(dz, dy, number).start()

    def wait_recv(self):
        for number, (dz, dy) in enumerate(neighbours()):

            @pl.when(self.there(-dz, -dy)[0])
            def _():
                self.copy(dz, dy, number).wait_recv()

    def wait_send(self):
        for number, (dz, dy) in enumerate(neighbours()):

            @pl.when(self.there(dz, dy)[0])
            def _():
                self.copy(dz, dy, number).wait_send()


class Plane:
    def __init__(self, n_gz, n_xy, n_x):
        gz, xy = lax.axis_index("gz"), lax.axis_index("xy")
        self.n_x = n_x
        self.members, self.levels = n_gz * n_x, n_xy // n_x
        self.level, self.x = lax.div(xy, n_x), lax.rem(xy, n_x)
        self.me = gz * n_x + self.x
        self.gz = gz

    def member(self, step):
        who = lax.rem(self.me + step, self.members)
        return who, (lax.div(who, self.n_x), self.level * self.n_x + lax.rem(who, self.n_x))

    def above(self, step):
        level = lax.rem(self.level + step, self.levels)
        return self.gz, level * self.n_x + self.x


def each(count, action):
    def one(step, carry):
        action(step)
        return carry

    lax.fori_loop(1, count, one, 0)


class Total:
    def __init__(self, plane, sums, got, level_got, out, sems):
        self.plane, self.sums, self.got, self.level_got, self.out = plane, sums, got, level_got, out
        self.sems = sems
        self.chunk = got.shape[1]
        self.own = pl.ds(pl.multiple_of(plane.me * self.chunk, self.chunk), self.chunk)

    def remote(self, stage, step, source, target, device):
        return pltpu.make_async_remote_copy(
            src_ref=source,
            dst_ref=target,
            send_sem=self.sems[2 * stage].at[step],
            recv_sem=self.sems[2 * stage + 1].at[step],
            device_id=device,
            device_id_type=MESH,
        )

    def scatter(self, step):
        who, device = self.plane.member(step)
        part = pl.ds(pl.multiple_of(who * self.chunk, self.chunk), self.chunk)
        return self.remote(0, step, self.sums.at[part], self.got.at[step], device)

    def column(self, step):
        here = self.level_got.at[self.plane.level]
        return self.remote(1, step, here, here, self.plane.above(step))

    def gather(self, step):
        here = self.out.at[self.own]
        return self.remote(2, step, here, here, self.plane.member(step)[1])

    def start(self):
        each(self.plane.members, lambda step: self.scatter(step).start())

    def middle(self):
        each(self.plane.members, lambda step: self.scatter(step).wait_recv())
        total = self.sums[self.own, :].astype(F32)
        for step in range(1, self.plane.members):
            total = total + self.got[step].astype(F32)
        self.level_got[self.plane.level] = total.astype(BF16)
        each(self.plane.levels, lambda step: self.column(step).start())

    def spread(self):
        each(self.plane.levels, lambda step: self.column(step).wait_recv())
        total = self.level_got[0].astype(F32)
        for level in range(1, self.plane.levels):
            total = total + self.level_got[level].astype(F32)
        self.out[self.own, :] = total.astype(BF16)
        each(self.plane.members, lambda step: self.gather(step).start())

    def finish(self):
        each(self.plane.members, lambda step: self.gather(step).wait_recv())

    def drain(self):
        each(self.plane.members, lambda step: self.scatter(step).wait_send())
        each(self.plane.levels, lambda step: self.column(step).wait_send())
        each(self.plane.members, lambda step: self.gather(step).wait_send())


def weight_halves(weight, half, turned):
    lows, highs = [], []
    count = weight.shape[1] // half
    for first in range(0, count, 2):
        if first + 1 < count:
            near = weight[:, pl.ds(first * half, 2 * half)].astype(F32)
        else:
            last = weight[:, pl.ds(first * half, half)].astype(F32)
            near = jnp.concatenate([last, jnp.zeros_like(last)], axis=1)
        far = pltpu.roll(near, half, 1)
        if turned:
            both = jnp.concatenate([near, far], axis=0).T
            near, far = both[:half], both[half:]
        lows += [near, far]
        highs += [far, near]
    return lows, highs


def fill_band(target, weight, turned):
    half = weight.shape[0]
    lows, highs = weight_halves(weight, half, turned)
    low = lax.broadcasted_iota(jnp.int32, (half, 2 * half), 1) < half
    for offset in range(9):
        ks = [26 - 3 * offset - x if turned else 3 * offset + x for x in range(3)]
        parts = [
            jnp.where(low, lows[ks[1]], highs[ks[0]]),
            jnp.where(low, lows[ks[2]], highs[ks[1]]),
            jnp.where(low, 0.0, highs[ks[2]]),
            jnp.where(low, lows[ks[0]], 0.0),
        ]
        for place, part in enumerate(parts):
            target[pl.ds((4 * offset + place) * half, half), :] = part.astype(BF16)


def side_lanes(cells, half, period):
    pairs = cells.shape[1]
    lane = lax.broadcasted_iota(jnp.int32, cells.shape, 2)
    place = lax.broadcasted_iota(jnp.int32, cells.shape, 1) % period
    right = pltpu.roll(cells, pairs - 1, 1)
    left = pltpu.roll(cells, 1, 1)
    low = lane < half
    right = jnp.where(place == period - 1, 0.0, right)
    left = jnp.where(place == 0, 0.0, left)
    return jnp.where(low, right, left)


def fill_windows(target, source, half, period, inner):
    depth = target.shape[0]
    lanes = 2 * half
    if inner:
        target[...] = jnp.zeros_like(target)
    first, last = (1, depth - 1) if inner else (0, depth)
    for z in range(first, last):
        cells = source(z - first)
        rows = pl.ds(1, target.shape[1] - 2) if inner else pl.ds(0, target.shape[1])
        target[z, rows, :, pl.ds(0, lanes)] = cells.astype(BF16)
        target[z, rows, :, pl.ds(lanes, lanes)] = side_lanes(cells.astype(F32), half, period).astype(
            BF16
        )


def window_rows(windows, z, count, dz, dy):
    rows = windows.shape[1] - 2
    pairs, width = windows.shape[2], windows.shape[3]
    part = windows[pl.ds(z + dz, count), pl.ds(dy, rows)]
    return part.reshape(count * rows * pairs, width)


def conv_rows(windows, weight, z, count):
    parts = [window_rows(windows, z, count, dz, dy) for dz in range(3) for dy in range(3)]
    return jnp.dot(jnp.concatenate(parts, axis=1), weight[...], preferred_element_type=F32)


def outer_sums(out, base, windows, grad_turned, half):
    depth = windows.shape[0] - 2
    lanes = 2 * half
    lane = lax.broadcasted_iota(jnp.int32, (half, lanes), 1)
    held = None
    for offset in range(9):
        both = jnp.dot(
            grad_turned,
            window_rows(windows, 0, depth, offset // 3, offset % 3),
            preferred_element_type=F32,
        )
        top_near, top_far = both[:half, :lanes], both[:half, lanes:]
        far_turned = pltpu.roll(top_far, half, 1)
        near_turned = pltpu.roll(top_near, half, 1)
        first = jnp.where(lane < half, far_turned, near_turned) + both[half:, :lanes]
        third = near_turned + both[half:, lanes:]
        out[pl.ds(base + offset * half, half), :] = first.astype(BF16)
        if offset % 2 == 0:
            held = jnp.where(lane < half, third, 0.0)
        else:
            pair = held + jnp.where(lane < half, 0.0, pltpu.roll(third, half, 1))
            out[pl.ds(base + (9 + offset // 2) * half, half), :] = pair.astype(BF16)
    out[pl.ds(base + 13 * half, half), :] = held.astype(BF16)


def clear_frame(framed):
    depth, rows = framed.shape[0], framed.shape[1]
    for z in (0, depth - 1):
        framed[z] = jnp.zeros(framed.shape[1:], framed.dtype)
    side = (depth - 2, 1) + framed.shape[2:]
    for y in (0, rows - 1):
        framed[pl.ds(1, depth - 2), pl.ds(y, 1)] = jnp.zeros(side, framed.dtype)


def frame_sides(framed, half):
    depth, rows = framed.shape[0], framed.shape[1]
    pairs, lanes = framed.shape[2], 2 * half

    def fill(zs, ys):
        cells = framed[zs, ys, :, pl.ds(0, lanes)].reshape(-1, pairs, lanes).astype(F32)
        turned = side_lanes(cells, half, pairs).astype(BF16)
        framed[zs, ys, :, pl.ds(lanes, lanes)] = turned.reshape(zs.size, ys.size, pairs, lanes)

    for z in (0, depth - 1):
        fill(pl.ds(z, 1), pl.ds(0, rows))
    for y in (0, rows - 1):
        fill(pl.ds(1, depth - 2), pl.ds(y, 1))


def step_kernel(
    n_gz, n_xy, n_x, period,
    vol_h, cot_h, back_h, refine_h, mix_h, slot_h, count_h,
    vgrad_h, tot_a, tot_b,
    vin, cin, back, refine, mix, slot, count, vout,
    tall, cot, xw, fw, pw, gw, wb, wr, wrt, wbt, gate_s, pg_s,
    sum_a, sum_b, got_a, got_b, level_a, level_b,
    local, rim_send, rim_recv, grad_send, grad_recv, *sems,
):
    depth, pairs, rows, lanes = vin.shape
    half = lanes // 2
    slots, tiles = cin.shape[0], pairs // period
    capacity = slot.shape[0]
    step = 4 if depth % 4 == 0 else depth
    flat = step * rows * pairs
    block = 14 * half
    gz, xy = lax.axis_index("gz"), lax.axis_index("xy")
    place, sizes = (gz, xy), (n_gz, n_xy)
    plane = Plane(n_gz, n_xy, n_x)
    rims = Rims(sizes, place, xw, depth, rows, lanes, rim_send, rim_recv)
    grad_rims = Rims(sizes, place, gw, depth, rows, lanes, grad_send, grad_recv)
    total_a = Total(plane, sum_a, got_a, level_a, tot_a, sems[:6])
    total_b = Total(plane, sum_b, got_b, level_b, tot_b, sems[6:])

    loads = [
        pltpu.make_async_copy(source, target, local.at[number])
        for number, (source, target) in enumerate(
            (
                (vol_h, vin), (back_h, back), (refine_h, refine), (mix_h, mix),
                (slot_h, slot), (count_h, count), (cot_h, cin),
            )
        )
    ]
    for load in loads:
        load.start()
    for framed in (xw, gw, fw, pw):
        clear_frame(framed)

    barrier = pltpu.get_barrier_semaphore()

    def greet(device):
        pl.semaphore_signal(barrier, inc=1, device_id=device, device_id_type=MESH)

    for dz, dy in neighbours():
        inside, where = rims.there(dz, dy)

        @pl.when(inside)
        def _():
            greet(where)

    each(plane.members, lambda step: greet(plane.member(step)[1]))
    each(plane.levels, lambda step: greet(plane.above(step)))

    loads[0].wait()

    def turn_in(z, carry):
        tall[pl.ds(pl.multiple_of(z * pairs * rows, 8), pairs * rows), :] = (
            vin[z].astype(F32).reshape(pairs * rows, lanes)
        )
        for y in range(rows):
            cells = tall[pl.ds(z * pairs * rows + y, pairs, stride=rows), :]
            xw[z + 1, y + 1, :, pl.ds(0, lanes)] = cells.astype(BF16)
        return carry

    lax.fori_loop(0, depth, turn_in, 0)

    across = 1 + lax.min(gz, 1) + lax.min(n_gz - 1 - gz, 1)
    along = 1 + lax.min(xy, 1) + lax.min(n_xy - 1 - xy, 1)
    pl.semaphore_wait(barrier, across * along - 1 + plane.members - 1 + plane.levels - 1)
    rims.start()

    inner = pl.ds(1, rows)

    def own_sides(z, carry):
        cells = xw[z + 1, inner, :, pl.ds(0, lanes)].astype(F32)
        xw[z + 1, inner, :, pl.ds(lanes, lanes)] = side_lanes(cells, half, pairs).astype(BF16)
        return carry

    lax.fori_loop(0, depth, own_sides, 0)
    loads[1].wait()
    fill_band(wb, back, False)
    loads[2].wait()
    fill_band(wr, refine, False)
    fill_band(wrt, refine, True)
    fill_band(wbt, back, True)
    loads[3].wait()
    mixed = mix[...].astype(F32)
    mixed = jnp.concatenate([mixed, jnp.zeros_like(mixed)], axis=1)
    mix2 = jnp.concatenate([mixed, pltpu.roll(mixed, half, 1)], axis=0).T.astype(BF16)

    for load in loads[4:]:
        load.wait()
    picks = []
    for number in range(slots):
        owner, place_in = number // capacity, number % capacity
        live = place_in < count[xy, owner]
        which = slot[place_in, owner]
        picks.append([jnp.where(live & (which == tile), 1.0, 0.0) for tile in range(tiles)])

    def pick(z, carry):
        held = [None] * tiles
        for number in range(slots):
            cells = cin[number, z].astype(F32)
            for tile in range(tiles):
                term = cells * picks[number][tile]
                held[tile] = term if held[tile] is None else held[tile] + term
        span = period * rows
        for tile in range(tiles):
            start = pl.multiple_of(z * pairs * rows + tile * span, 8)
            tall[pl.ds(start, span), :] = held[tile].reshape(span, lanes)
        for y in range(rows):
            cot[z, y] = tall[pl.ds(z * pairs * rows + y, pairs, stride=rows), :]
        return carry

    lax.fori_loop(0, depth, pick, 0)

    rims.wait_recv()
    frame_sides(xw, half)

    def put(target, z, cells, period):
        target[pl.ds(z + 1, step), inner, :, pl.ds(0, lanes)] = cells.astype(BF16)
        close = cells.astype(F32).reshape(step * rows, pairs, lanes)
        target[pl.ds(z + 1, step), inner, :, pl.ds(lanes, lanes)] = (
            side_lanes(close, half, period).astype(BF16).reshape(step, rows, pairs, lanes)
        )

    brick = (step, rows, pairs, lanes)
    for z in range(0, depth, step):
        own = xw[pl.ds(z + 1, step), inner, :, pl.ds(0, lanes)].astype(F32).reshape(flat, lanes)
        feature = (own + conv_rows(xw, wb, z, step)).astype(BF16)
        put(fw, z, feature.reshape(brick), period)
    for z in range(0, depth, step):
        pre = conv_rows(fw, wr, z, step)
        sig = jax.nn.sigmoid(pre)
        upstream = cot[pl.ds(z, step)].reshape(flat, lanes).astype(BF16)
        gate_s[pl.ds(z * rows * pairs, flat), :] = (pre * sig).astype(BF16)
        gated_grad = jnp.dot(upstream, mix2, preferred_element_type=F32)
        pre_grad = (gated_grad * sig * (1.0 + pre * (1.0 - sig))).astype(BF16)
        pg_s[pl.ds(z * rows * pairs, flat), :] = pre_grad
        put(pw, z, pre_grad.reshape(brick), period)

    outer_sums(sum_a, 0, fw, pg_s[...].T, half)
    cot_rows = cot[...].reshape(depth * rows * pairs, lanes).astype(BF16)
    both = jnp.dot(gate_s[...].T, cot_rows, preferred_element_type=F32)
    lane = lax.broadcasted_iota(jnp.int32, (half, lanes), 1)
    sum_a[pl.ds(block, half), :] = jnp.where(
        lane < half, both[:half] + pltpu.roll(both[half:], half, 1), 0.0
    ).astype(BF16)
    used = block + half
    if used < sum_a.shape[0]:
        sum_a[pl.ds(used, sum_a.shape[0] - used), :] = jnp.zeros((sum_a.shape[0] - used, lanes), BF16)
    total_a.start()

    for z in range(0, depth, step):
        upstream = cot[pl.ds(z, step)].reshape(flat, lanes)
        grad = (upstream + conv_rows(pw, wrt, z, step)).astype(BF16)
        put(gw, z, grad.reshape(brick), pairs)
    grad_rims.start()

    own = gw[pl.ds(1, depth), inner, :, pl.ds(0, lanes)].reshape(depth * rows * pairs, lanes)
    outer_sums(sum_b, 0, xw, own.T, half)
    if block < sum_b.shape[0]:
        sum_b[pl.ds(block, sum_b.shape[0] - block), :] = jnp.zeros((sum_b.shape[0] - block, lanes), BF16)
    total_b.start()
    total_a.middle()

    grad_rims.wait_recv()
    frame_sides(gw, half)

    def back_conv(z):
        own = gw[pl.ds(z + 1, step), inner, :, pl.ds(0, lanes)].astype(F32).reshape(flat, lanes)
        tall[pl.ds(z * rows * pairs, flat), :] = own + conv_rows(gw, wbt, z, step)

    back_conv(0)
    total_b.middle()
    for z in range(step, depth, step):
        back_conv(z)
    total_a.spread()

    def turn_out(z, carry):
        for pair in range(pairs):
            cells = tall[pl.ds(z * pairs * rows + pair, rows, stride=pairs), :]
            vout[z, pair] = cells.astype(BF16)
        return carry

    lax.fori_loop(0, depth, turn_out, 0)
    store = pltpu.make_async_copy(vout, vgrad_h, local.at[len(loads)])
    store.start()
    total_b.spread()
    total_a.finish()
    total_b.finish()
    rims.wait_send()
    grad_rims.wait_send()
    total_a.drain()
    total_b.drain()
    store.wait()


def finish_kernel(tot_a, tot_b, back_step, refine_step, mix_step):
    half = mix_step.shape[0]
    lanes = 2 * half
    block = 14 * half
    low = lax.broadcasted_iota(jnp.int32, (half, lanes), 1) < half

    def scale_of(values, count):
        squares = jnp.sum(values * values, axis=0, keepdims=True)
        return jnp.sqrt(jnp.sum(squares, axis=1, keepdims=True) / count + EPSILON)

    for totals, out in ((tot_b, back_step), (tot_a, refine_step)):
        values = totals[pl.ds(0, block), :].astype(F32)
        scale = scale_of(values, 27.0 * half * half)
        lows, highs = [None] * 28, [None] * 28
        for tile in range(14):
            near = values[tile * half : (tile + 1) * half]
            both = jnp.concatenate([near, pltpu.roll(near, half, 1)], axis=0).T / scale
            if tile < 9:
                first, second = 3 * tile, 3 * tile + 1
            else:
                first, second = 6 * (tile - 9) + 2, 6 * (tile - 9) + 5
            lows[first], highs[first] = both[:half], both[half:]
            if second < 27:
                lows[second], highs[second] = both[half:], both[:half]
        for k in range(0, 26, 2):
            out[:, pl.ds(k * half, lanes)] = jnp.where(low, lows[k], highs[k + 1])
        out[:, pl.ds(26 * half, half)] = lows[26][:, :half]
    values = tot_a[pl.ds(block, half), :].astype(F32)
    mix_step[...] = (values / scale_of(values, 1.0 * half * half))[:, :half]


def body(volume, backbone_weight, refine_weight, mix_weight, tile_cot, tile_slot, tile_count):
    depth, rows, width = volume.shape
    channels = mix_weight.shape[0]
    edge = tile_cot.shape[4]
    owners, capacity = tile_cot.shape[2], tile_cot.shape[3]
    assert depth == edge and rows == edge
    lanes = 2 * channels
    pairs = width // lanes
    period = edge // 2
    slots = owners * capacity
    n_gz, n_xy = lax.axis_size("gz"), lax.axis_size("xy")
    n_x = max(n_gz // 2, 1)
    if n_xy % n_x:
        n_x = 1
    members, levels = n_gz * n_x, n_xy // n_x

    vol = volume.reshape(depth, rows, pairs, lanes).transpose(0, 2, 1, 3)
    cot = tile_cot.reshape(slots, edge, edge, period, lanes).transpose(0, 1, 3, 2, 4)
    slot = tile_slot.reshape(owners, capacity).T
    count = tile_count.reshape(owners, owners)

    block = 14 * channels
    chunk_a = -(-(block + channels) // (members * 16)) * 16
    chunk_b = -(-block // (members * 16)) * 16
    framed = pltpu.VMEM((depth + 2, rows + 2, pairs, 2 * lanes), BF16)
    band = pltpu.VMEM((36 * channels, lanes), BF16)
    cells = depth * rows * pairs
    dma = pltpu.SemaphoreType.DMA
    vgrad, tot_a, tot_b = pl.pallas_call(
        functools.partial(step_kernel, n_gz, n_xy, n_x, period),
        out_shape=(
            jax.ShapeDtypeStruct(vol.shape, BF16),
            jax.ShapeDtypeStruct((members * chunk_a, lanes), BF16),
            jax.ShapeDtypeStruct((members * chunk_b, lanes), BF16),
        ),
        in_specs=[ANY] * 7,
        out_specs=(ANY, VMEM, VMEM),
        scratch_shapes=[
            pltpu.VMEM(vol.shape, BF16),
            pltpu.VMEM(cot.shape, BF16),
            pltpu.VMEM(backbone_weight.shape, BF16),
            pltpu.VMEM(refine_weight.shape, BF16),
            pltpu.VMEM(mix_weight.shape, BF16),
            pltpu.SMEM(slot.shape, jnp.int32),
            pltpu.SMEM(count.shape, jnp.int32),
            pltpu.VMEM(vol.shape, BF16),
            pltpu.VMEM((cells, lanes), F32),
            pltpu.VMEM((depth, rows, pairs, lanes), F32),
            framed, framed, framed, framed,
            band, band, band, band,
            pltpu.VMEM((cells, lanes), BF16),
            pltpu.VMEM((cells, lanes), BF16),
            pltpu.VMEM((members * chunk_a, lanes), BF16),
            pltpu.VMEM((members * chunk_b, lanes), BF16),
            pltpu.VMEM((members, chunk_a, lanes), BF16),
            pltpu.VMEM((members, chunk_b, lanes), BF16),
            pltpu.VMEM((levels, chunk_a, lanes), BF16),
            pltpu.VMEM((levels, chunk_b, lanes), BF16),
            dma((8,)),
            dma((8,)), dma((8,)), dma((8,)), dma((8,)),
        ]
        + [dma((n,)) for n in (members, members, levels, levels, members, members)] * 2,
        compiler_params=pltpu.CompilerParams(
            collective_id=0, has_side_effects=True, vmem_limit_bytes=56 * 1024 * 1024
        ),
    )(vol, cot, backbone_weight, refine_weight, mix_weight, slot, count)
    wide = jax.ShapeDtypeStruct((channels, 27 * channels), F32)
    back_step, refine_step, mix_step = pl.pallas_call(
        finish_kernel,
        out_shape=(wide, wide, jax.ShapeDtypeStruct((channels, channels), F32)),
        in_specs=[VMEM] * 2,
        out_specs=(VMEM,) * 3,
    )(tot_a, tot_b)
    vgrad = vgrad.transpose(0, 2, 1, 3).reshape(depth, rows, width)
    return (vgrad, back_step, refine_step, mix_step)


def solution(mesh):
    in_specs = (
        P("gz", "xy", None),
        P(),
        P(),
        P(),
        P("gz", "xy", None, None, None, None, None),
        P("gz", "xy", None, None),
        P("gz", None, None),
    )
    out_specs = (P("gz", "xy", None), P(), P(), P())
    return jax.shard_map(body, mesh=mesh, in_specs=in_specs, out_specs=out_specs, check_vma=False)
```

```python
import functools

import jax
import jax.numpy as jnp
from jax import lax
from jax.experimental import pallas as pl
from jax.experimental.pallas import tpu as pltpu
from jax.sharding import PartitionSpec as P

EPSILON = 1e-06
F32 = jnp.float32
BF16 = jnp.bfloat16
VMEM = pl.BlockSpec(memory_space=pltpu.VMEM)
ANY = pl.BlockSpec(memory_space=pl.ANY)
HBM = pl.BlockSpec(memory_space=pltpu.HBM)
MESH = pl.DeviceIdType.MESH


def neighbours():
    return [(dz, dy) for dz in (-1, 0, 1) for dy in (-1, 0, 1) if (dz, dy) != (0, 0)]


def near(step, size):
    if step == 0:
        return pl.ds(1, size)
    return pl.ds(size, 1) if step > 0 else pl.ds(1, 1)


def far(step, size):
    if step == 0:
        return pl.ds(1, size)
    return pl.ds(0, 1) if step > 0 else pl.ds(size + 1, 1)


class Rims:
    def __init__(self, sizes, place, framed, depth, rows, lanes, send, recv):
        self.sizes, self.place, self.framed = sizes, place, framed
        self.depth, self.rows, self.lanes = depth, rows, lanes
        self.send, self.recv = send, recv

    def there(self, dz, dy):
        (n_gz, n_xy), (gz, xy) = self.sizes, self.place
        inside = (gz + dz >= 0) & (gz + dz < n_gz) & (xy + dy >= 0) & (xy + dy < n_xy)
        return inside, (gz + dz, xy + dy)

    def copy(self, dz, dy, number):
        cells = (slice(None), pl.ds(0, self.lanes))
        return pltpu.make_async_remote_copy(
            src_ref=self.framed.at[(near(dz, self.depth), near(dy, self.rows)) + cells],
            dst_ref=self.framed.at[(far(dz, self.depth), far(dy, self.rows)) + cells],
            send_sem=self.send.at[number],
            recv_sem=self.recv.at[number],
            device_id=self.there(dz, dy)[1],
            device_id_type=MESH,
        )

    def start(self):
        for number, (dz, dy) in enumerate(neighbours()):

            @pl.when(self.there(dz, dy)[0])
            def _():
                self.copy(dz, dy, number).start()

    def wait_recv(self):
        for number, (dz, dy) in enumerate(neighbours()):

            @pl.when(self.there(-dz, -dy)[0])
            def _():
                self.copy(dz, dy, number).wait_recv()

    def wait_send(self):
        for number, (dz, dy) in enumerate(neighbours()):

            @pl.when(self.there(dz, dy)[0])
            def _():
                self.copy(dz, dy, number).wait_send()


class Plane:
    def __init__(self, n_gz, n_xy, n_x):
        gz, xy = lax.axis_index("gz"), lax.axis_index("xy")
        self.n_x = n_x
        self.members, self.levels = n_gz * n_x, n_xy // n_x
        self.level, self.x = lax.div(xy, n_x), lax.rem(xy, n_x)
        self.me = gz * n_x + self.x
        self.gz = gz

    def member(self, step):
        who = lax.rem(self.me + step, self.members)
        return who, (lax.div(who, self.n_x), self.level * self.n_x + lax.rem(who, self.n_x))

    def above(self, step):
        level = lax.rem(self.level + step, self.levels)
        return self.gz, level * self.n_x + self.x


def each(count, action):
    def one(step, carry):
        action(step)
        return carry

    lax.fori_loop(1, count, one, 0)


class Total:
    def __init__(self, plane, sums, got, level_got, out, sems):
        self.plane, self.sums, self.got, self.level_got, self.out = plane, sums, got, level_got, out
        self.sems = sems
        self.chunk = got.shape[1]
        self.own = pl.ds(pl.multiple_of(plane.me * self.chunk, self.chunk), self.chunk)

    def remote(self, stage, step, source, target, device):
        return pltpu.make_async_remote_copy(
            src_ref=source,
            dst_ref=target,
            send_sem=self.sems[2 * stage].at[step],
            recv_sem=self.sems[2 * stage + 1].at[step],
            device_id=device,
            device_id_type=MESH,
        )

    def scatter(self, step):
        who, device = self.plane.member(step)
        part = pl.ds(pl.multiple_of(who * self.chunk, self.chunk), self.chunk)
        return self.remote(0, step, self.sums.at[part], self.got.at[step], device)

    def column(self, step):
        here = self.level_got.at[self.plane.level]
        return self.remote(1, step, here, here, self.plane.above(step))

    def gather(self, step):
        here = self.out.at[self.own]
        return self.remote(2, step, here, here, self.plane.member(step)[1])

    def start(self):
        each(self.plane.members, lambda step: self.scatter(step).start())

    def middle(self):
        each(self.plane.members, lambda step: self.scatter(step).wait_recv())
        total = self.sums[self.own, :].astype(F32)
        for step in range(1, self.plane.members):
            total = total + self.got[step].astype(F32)
        self.level_got[self.plane.level] = total.astype(BF16)
        each(self.plane.levels, lambda step: self.column(step).start())

    def spread(self):
        each(self.plane.levels, lambda step: self.column(step).wait_recv())
        total = self.level_got[0].astype(F32)
        for level in range(1, self.plane.levels):
            total = total + self.level_got[level].astype(F32)
        self.out[self.own, :] = total.astype(BF16)
        each(self.plane.members, lambda step: self.gather(step).start())

    def finish(self):
        each(self.plane.members, lambda step: self.gather(step).wait_recv())

    def drain(self):
        each(self.plane.members, lambda step: self.scatter(step).wait_send())
        each(self.plane.levels, lambda step: self.column(step).wait_send())
        each(self.plane.members, lambda step: self.gather(step).wait_send())


def weight_halves(weight, half, turned):
    lows, highs = [], []
    count = weight.shape[1] // half
    for first in range(0, count, 2):
        if first + 1 < count:
            near = weight[:, pl.ds(first * half, 2 * half)].astype(F32)
        else:
            last = weight[:, pl.ds(first * half, half)].astype(F32)
            near = jnp.concatenate([last, jnp.zeros_like(last)], axis=1)
        far = pltpu.roll(near, half, 1)
        if turned:
            both = jnp.concatenate([near, far], axis=0).T
            near, far = both[:half], both[half:]
        lows += [near, far]
        highs += [far, near]
    return lows, highs


def fill_band(target, weight, turned):
    half = weight.shape[0]
    lanes = 2 * half
    lows, highs = weight_halves(weight, half, turned)
    low = lax.broadcasted_iota(jnp.int32, (half, lanes), 1) < half
    for offset in range(9):
        ks = [26 - 3 * offset - x if turned else 3 * offset + x for x in range(3)]
        parts = [
            jnp.where(low, lows[ks[1]], highs[ks[0]]),
            jnp.where(low, lows[ks[2]], highs[ks[1]]),
            jnp.where(low, 0.0, highs[ks[2]]),
            jnp.where(low, lows[ks[0]], 0.0),
        ]
        tile = 4 * (offset // 3) + offset % 3
        for place, part in enumerate(parts):
            part = part.astype(BF16)
            target[pl.ds((4 * tile + place) * half, half), pl.ds(0, lanes)] = part
            target[pl.ds((4 * tile + 4 + place) * half, half), pl.ds(lanes, lanes)] = part
    empty = jnp.zeros((4 * half, lanes), BF16)
    for dz in range(3):
        target[pl.ds((4 * dz + 3) * 4 * half, 4 * half), pl.ds(0, lanes)] = empty
        target[pl.ds(4 * dz * 4 * half, 4 * half), pl.ds(lanes, lanes)] = empty


def side_lanes(cells, half, period):
    pairs = cells.shape[1]
    lane = lax.broadcasted_iota(jnp.int32, cells.shape, 2)
    place = lax.broadcasted_iota(jnp.int32, cells.shape, 1) % period
    right = pltpu.roll(cells, pairs - 1, 1)
    left = pltpu.roll(cells, 1, 1)
    low = lane < half
    right = jnp.where(place == period - 1, 0.0, right)
    left = jnp.where(place == 0, 0.0, left)
    return jnp.where(low, right, left)


def window_rows(windows, z, count, dz, dy):
    pairs, width = windows.shape[2], windows.shape[3]
    parts = [
        windows[pl.ds(z + dz, count), y + dy].reshape(count * pairs, width)
        for y in range(0, windows.shape[1] - 2, 2)
    ]
    return jnp.concatenate(parts, axis=0)


def conv_rows(windows, weight, z, count):
    parts = [window_rows(windows, z, count, dz, dy) for dz in range(3) for dy in range(4)]
    return jnp.dot(jnp.concatenate(parts, axis=1), weight[...], preferred_element_type=F32)


def outer_sums(out, windows, grad_turned, half, step):
    depth = windows.shape[0] - 2
    lanes = 2 * half
    low = lax.broadcasted_iota(jnp.int32, (half, lanes), 1) < half
    held = {}

    def turn(values):
        return pltpu.roll(values, half, 1)

    for dz in range(3):
        products = []
        for dy in range(4):
            seen = [window_rows(windows, z, step, dz, dy) for z in range(0, depth, step)]
            seen = jnp.concatenate(seen, axis=0)
            products.append(jnp.dot(grad_turned, seen, preferred_element_type=F32))
        for dy in range(3):
            both = products[dy][:lanes] + products[dy + 1][lanes:]
            top_near, top_far = both[:half, :lanes], both[:half, lanes:]
            last_near, last_far = both[half:, :lanes], both[half:, lanes:]
            sums = ((top_far, last_near), (last_near, top_near), (top_near, last_far))
            for dx, (right, left) in enumerate(sums):
                k = 3 * (3 * dz + dy) + dx
                tile = 2 * (k // 4) + k % 2
                if k % 4 < 2:
                    held[tile] = turn(right) + left
                else:
                    pair = jnp.where(low, held.pop(tile), right + turn(left))
                    out[pl.ds(tile * half, half), :] = pair.astype(BF16)
    for tile, values in held.items():
        out[pl.ds(tile * half, half), :] = jnp.where(low, values, 0.0).astype(BF16)


def clear_frame(framed):
    depth, rows = framed.shape[0], framed.shape[1]
    for z in (0, depth - 1):
        framed[z] = jnp.zeros(framed.shape[1:], framed.dtype)
    side = (depth - 2, 1) + framed.shape[2:]
    for y in (0, rows - 1):
        framed[pl.ds(1, depth - 2), pl.ds(y, 1)] = jnp.zeros(side, framed.dtype)


def frame_sides(framed, half):
    depth, rows = framed.shape[0], framed.shape[1]
    pairs, lanes = framed.shape[2], 2 * half

    def fill(zs, ys):
        cells = framed[zs, ys, :, pl.ds(0, lanes)].reshape(-1, pairs, lanes).astype(F32)
        turned = side_lanes(cells, half, pairs).astype(BF16)
        framed[zs, ys, :, pl.ds(lanes, lanes)] = turned.reshape(zs.size, ys.size, pairs, lanes)

    for z in (0, depth - 1):
        fill(pl.ds(z, 1), pl.ds(0, rows))
    for y in (0, rows - 1):
        fill(pl.ds(1, depth - 2), pl.ds(y, 1))


def step_kernel(
    n_gz, n_xy, n_x, period,
    vol_h, cot_h, back_h, refine_h, mix_h, slot_h, count_h,
    vgrad, tot_b, refine_step, mix_step,
    vin, cin, back, refine, mix, slot, count,
    tall, cot, xw, fw, pw, gw, wb, wr, wrt, wbt, gate_s, pg_s, own_s,
    tot_a, sum_a, sum_b, got_a, got_b, level_a, level_b,
    local, rim_send, rim_recv, grad_send, grad_recv, *sems,
):
    depth, pairs, rows, lanes = vin.shape
    half = lanes // 2
    slots, tiles = cin.shape[0], pairs // period
    capacity = slot.shape[0]
    step = 4 if depth % 4 == 0 else depth
    couples = rows // 2
    flat = step * couples * pairs
    block = 14 * half
    gz, xy = lax.axis_index("gz"), lax.axis_index("xy")
    place, sizes = (gz, xy), (n_gz, n_xy)
    plane = Plane(n_gz, n_xy, n_x)
    rims = Rims(sizes, place, xw, depth, rows, lanes, rim_send, rim_recv)
    grad_rims = Rims(sizes, place, gw, depth, rows, lanes, grad_send, grad_recv)
    total_a = Total(plane, sum_a, got_a, level_a, tot_a, sems[:6])
    total_b = Total(plane, sum_b, got_b, level_b, tot_b, sems[6:])

    loads = [
        pltpu.make_async_copy(source, target, local.at[number])
        for number, (source, target) in enumerate(
            (
                (vol_h, vin), (back_h, back), (refine_h, refine), (mix_h, mix),
                (slot_h, slot), (count_h, count), (cot_h, cin),
            )
        )
    ]
    for load in loads:
        load.start()
    for framed in (xw, gw, fw, pw):
        clear_frame(framed)

    barrier = pltpu.get_barrier_semaphore()

    def greet(device):
        pl.semaphore_signal(barrier, inc=1, device_id=device, device_id_type=MESH)

    for dz, dy in neighbours():
        inside, where = rims.there(dz, dy)

        @pl.when(inside)
        def _():
            greet(where)

    each(plane.members, lambda step: greet(plane.member(step)[1]))
    each(plane.levels, lambda step: greet(plane.above(step)))

    loads[0].wait()

    def turn_in(z, carry):
        tall[pl.ds(pl.multiple_of(z * pairs * rows, 8), pairs * rows), :] = (
            vin[z].astype(F32).reshape(pairs * rows, lanes)
        )
        for y in range(rows):
            cells = tall[pl.ds(z * pairs * rows + y, pairs, stride=rows), :]
            xw[z + 1, y + 1, :, pl.ds(0, lanes)] = cells.astype(BF16)
        return carry

    lax.fori_loop(0, depth, turn_in, 0)

    across = 1 + lax.min(gz, 1) + lax.min(n_gz - 1 - gz, 1)
    along = 1 + lax.min(xy, 1) + lax.min(n_xy - 1 - xy, 1)
    pl.semaphore_wait(barrier, across * along - 1 + plane.members - 1 + plane.levels - 1)
    rims.start()

    inner = pl.ds(1, rows)

    def own_sides(z, carry):
        cells = xw[z + 1, inner, :, pl.ds(0, lanes)].astype(F32)
        xw[z + 1, inner, :, pl.ds(lanes, lanes)] = side_lanes(cells, half, pairs).astype(BF16)
        return carry

    lax.fori_loop(0, depth, own_sides, 0)
    loads[1].wait()
    fill_band(wb, back, False)
    loads[2].wait()
    fill_band(wr, refine, False)
    fill_band(wrt, refine, True)
    fill_band(wbt, back, True)
    loads[3].wait()
    mixed = mix[...].astype(F32)
    mixed = jnp.concatenate([mixed, jnp.zeros_like(mixed)], axis=1)
    mix2 = jnp.concatenate([mixed, pltpu.roll(mixed, half, 1)], axis=0).T
    blank = jnp.zeros_like(mix2)
    mix4 = jnp.concatenate(
        [jnp.concatenate([mix2, blank], axis=1), jnp.concatenate([blank, mix2], axis=1)], axis=0
    ).astype(BF16)

    for load in loads[4:]:
        load.wait()
    picks = []
    for number in range(slots):
        owner, place_in = number // capacity, number % capacity
        live = place_in < count[xy, owner]
        which = slot[place_in, owner]
        picks.append([jnp.where(live & (which == tile), 1.0, 0.0) for tile in range(tiles)])

    def pick(z, carry):
        held = [None] * tiles
        for number in range(slots):
            cells = cin[number, z].astype(F32)
            for tile in range(tiles):
                term = cells * picks[number][tile]
                held[tile] = term if held[tile] is None else held[tile] + term
        span = period * rows
        for tile in range(tiles):
            start = pl.multiple_of(z * pairs * rows + tile * span, 8)
            tall[pl.ds(start, span), :] = held[tile].reshape(span, lanes)
        for y in range(rows):
            cot[lax.div(z, step), y // 2, lax.rem(z, step), :, pl.ds(y % 2 * lanes, lanes)] = tall[
                pl.ds(z * pairs * rows + y, pairs, stride=rows), :
            ]
        return carry

    lax.fori_loop(0, depth, pick, 0)

    rims.wait_recv()
    frame_sides(xw, half)

    def put(target, z, cells, period):
        for y in range(rows):
            odd, first = y % 2, y // 2 * step * pairs
            own = cells[first : first + step * pairs, odd * lanes : (odd + 1) * lanes]
            own = own.reshape(step, pairs, lanes)
            target[pl.ds(z + 1, step), y + 1, :, pl.ds(0, lanes)] = own
            target[pl.ds(z + 1, step), y + 1, :, pl.ds(lanes, lanes)] = side_lanes(
                own.astype(F32), half, period
            ).astype(BF16)

    def take(framed, z):
        parts = [framed[pl.ds(z + 1, step), y + 1, :, pl.ds(0, lanes)] for y in range(rows)]
        parts = [part.reshape(step * pairs, lanes) for part in parts]
        lines = [jnp.concatenate(parts[odd::2], axis=0) for odd in range(2)]
        return jnp.concatenate(lines, axis=1).astype(F32)

    def line(z):
        return pl.ds(z * couples * pairs, flat)

    for z in range(0, depth, step):
        put(fw, z, (take(xw, z) + conv_rows(xw, wb, z, step)).astype(BF16), period)
    for z in range(0, depth, step):
        pre = conv_rows(fw, wr, z, step)
        sig = jax.nn.sigmoid(pre)
        upstream = cot[z // step].reshape(flat, 2 * lanes).astype(BF16)
        gate_s[line(z), :] = (pre * sig).astype(BF16)
        gated_grad = jnp.dot(upstream, mix4, preferred_element_type=F32)
        pre_grad = (gated_grad * sig * (1.0 + pre * (1.0 - sig))).astype(BF16)
        pg_s[line(z), :] = pre_grad
        put(pw, z, pre_grad, period)

    outer_sums(sum_a, fw, pg_s[...].T, half, step)
    cot_rows = cot[...].reshape(depth * couples * pairs, 2 * lanes).astype(BF16)
    both = jnp.dot(gate_s[...].T, cot_rows, preferred_element_type=F32)
    both = both[:lanes, :lanes] + both[lanes:, lanes:]
    lane = lax.broadcasted_iota(jnp.int32, (half, lanes), 1)
    sum_a[pl.ds(block, half), :] = jnp.where(
        lane < half, both[:half] + pltpu.roll(both[half:], half, 1), 0.0
    ).astype(BF16)
    used = block + half
    if used < sum_a.shape[0]:
        sum_a[pl.ds(used, sum_a.shape[0] - used), :] = jnp.zeros((sum_a.shape[0] - used, lanes), BF16)
    total_a.start()

    for z in range(0, depth, step):
        upstream = cot[z // step].reshape(flat, 2 * lanes)
        grad = (upstream + conv_rows(pw, wrt, z, step)).astype(BF16)
        own_s[line(z), :] = grad
        put(gw, z, grad, pairs)
    grad_rims.start()

    outer_sums(sum_b, xw, own_s[...].T, half, step)
    if block < sum_b.shape[0]:
        sum_b[pl.ds(block, sum_b.shape[0] - block), :] = jnp.zeros((sum_b.shape[0] - block, lanes), BF16)
    total_b.start()
    total_a.middle()

    grad_rims.wait_recv()
    frame_sides(gw, half)

    def back_conv(z):
        grad = own_s[line(z), :].astype(F32) + conv_rows(gw, wbt, z, step)
        grad = grad.reshape(couples, step, pairs, 2 * lanes)
        for y in range(rows):
            for level in range(step):
                tall[pl.ds(((z + level) * rows + y) * pairs, pairs), :] = grad[
                    y // 2, level, :, y % 2 * lanes : (y % 2 + 1) * lanes
                ]

    back_conv(0)
    total_b.middle()
    for z in range(step, depth, step):
        back_conv(z)
    total_a.spread()

    def turn_out(z, carry):
        for pair in range(pairs):
            cells = tall[pl.ds(z * pairs * rows + pair, rows, stride=pairs), :]
            vgrad[z, pair] = cells.astype(BF16)
        return carry

    lax.fori_loop(0, depth, turn_out, 0)
    total_b.spread()
    total_a.finish()
    write_step(tot_a, refine_step, half)
    values = tot_a[pl.ds(block, half), :].astype(F32)
    mix_step[...] = (values / scale_of(values, 1.0 * half * half))[:, :half]
    total_b.finish()
    rims.wait_send()
    grad_rims.wait_send()
    total_a.drain()
    total_b.drain()


def scale_of(values, count):
    squares = jnp.sum(values * values, axis=0, keepdims=True)
    return jnp.sqrt(jnp.sum(squares, axis=1, keepdims=True) / count + EPSILON)


def write_step(totals, out, half):
    lanes = 2 * half
    values = totals[pl.ds(0, 14 * half), :].astype(F32)
    scale = scale_of(values, 27.0 * half * half)
    for quad in range(7):
        turned = values[quad * lanes : (quad + 1) * lanes].T / scale
        out[:, pl.ds(quad * 2 * lanes, lanes)] = turned[:half]
        wide = min(lanes, out.shape[1] - quad * 2 * lanes - lanes)
        out[:, pl.ds(quad * 2 * lanes + lanes, wide)] = turned[half:, :wide]


def finish_kernel(
    vgrad, refine_step, mix_step, tot_b, vgrad_out, back_out, refine_out, mix_out, back_step, sems
):
    copies = [
        pltpu.make_async_copy(source, target, sems.at[number])
        for number, (source, target) in enumerate(
            ((vgrad, vgrad_out), (refine_step, refine_out), (mix_step, mix_out), (back_step, back_out))
        )
    ]
    for copy in copies[:3]:
        copy.start()
    write_step(tot_b, back_step, mix_step.shape[0])
    copies[3].start()
    for copy in copies:
        copy.wait()


def body(volume, backbone_weight, refine_weight, mix_weight, tile_cot, tile_slot, tile_count):
    depth, rows, width = volume.shape
    channels = mix_weight.shape[0]
    edge = tile_cot.shape[4]
    owners, capacity = tile_cot.shape[2], tile_cot.shape[3]
    assert depth == edge and rows == edge and rows % 2 == 0
    lanes = 2 * channels
    pairs = width // lanes
    period = edge // 2
    slots = owners * capacity
    n_gz, n_xy = lax.axis_size("gz"), lax.axis_size("xy")
    n_x = max(n_gz // 2, 1)
    if n_xy % n_x:
        n_x = 1
    members, levels = n_gz * n_x, n_xy // n_x

    vol = volume.reshape(depth, rows, pairs, lanes).transpose(0, 2, 1, 3)
    cot = tile_cot.reshape(slots, edge, edge, period, lanes).transpose(0, 1, 3, 2, 4)
    slot = tile_slot.reshape(owners, capacity).T
    count = tile_count.reshape(owners, owners)

    block = 14 * channels
    chunk_a = -(-(block + channels) // (members * 16)) * 16
    chunk_b = -(-block // (members * 16)) * 16
    framed = pltpu.VMEM((depth + 2, rows + 2, pairs, 2 * lanes), BF16)
    band = pltpu.VMEM((48 * channels, 2 * lanes), BF16)
    wide = jax.ShapeDtypeStruct((channels, 27 * channels), F32)
    small = jax.ShapeDtypeStruct((channels, channels), F32)
    cells = depth * rows * pairs
    dma = pltpu.SemaphoreType.DMA
    step = 4 if depth % 4 == 0 else depth
    operands = (vol, cot, backbone_weight, refine_weight, mix_weight, slot, count)
    vgrad, tot_b, refine_step, mix_step = pl.pallas_call(
        functools.partial(step_kernel, n_gz, n_xy, n_x, period),
        out_shape=(
            jax.ShapeDtypeStruct(vol.shape, BF16),
            jax.ShapeDtypeStruct((members * chunk_b, lanes), BF16),
            wide,
            small,
        ),
        in_specs=[HBM] * 7,
        out_specs=(VMEM,) * 4,
        scratch_shapes=[
            pltpu.VMEM(vol.shape, BF16),
            pltpu.VMEM(cot.shape, BF16),
            pltpu.VMEM(backbone_weight.shape, BF16),
            pltpu.VMEM(refine_weight.shape, BF16),
            pltpu.VMEM(mix_weight.shape, BF16),
            pltpu.SMEM(slot.shape, jnp.int32),
            pltpu.SMEM(count.shape, jnp.int32),
            pltpu.VMEM((cells, lanes), F32),
            pltpu.VMEM((depth // step, rows // 2, step, pairs, 2 * lanes), F32),
            framed, framed, framed, framed,
            band, band, band, band,
            pltpu.VMEM((cells // 2, 2 * lanes), BF16),
            pltpu.VMEM((cells // 2, 2 * lanes), BF16),
            pltpu.VMEM((cells // 2, 2 * lanes), BF16),
            pltpu.VMEM((members * chunk_a, lanes), BF16),
            pltpu.VMEM((members * chunk_a, lanes), BF16),
            pltpu.VMEM((members * chunk_b, lanes), BF16),
            pltpu.VMEM((members, chunk_a, lanes), BF16),
            pltpu.VMEM((members, chunk_b, lanes), BF16),
            pltpu.VMEM((levels, chunk_a, lanes), BF16),
            pltpu.VMEM((levels, chunk_b, lanes), BF16),
            dma((8,)),
            dma((8,)), dma((8,)), dma((8,)), dma((8,)),
        ]
        + [dma((n,)) for n in (members, members, levels, levels, members, members)] * 2,
        compiler_params=pltpu.CompilerParams(
            collective_id=0, has_side_effects=True, vmem_limit_bytes=32 * 1024 * 1024
        ),
    )(*[pltpu.with_memory_space_constraint(operand, pltpu.HBM) for operand in operands])
    vgrad, back_step, refine_step, mix_step = pl.pallas_call(
        finish_kernel,
        out_shape=(jax.ShapeDtypeStruct(vol.shape, BF16), wide, wide, small),
        in_specs=[VMEM] * 4,
        out_specs=(ANY,) * 4,
        scratch_shapes=[pltpu.VMEM(wide.shape, F32), dma((4,))],
        compiler_params=pltpu.CompilerParams(vmem_limit_bytes=8 * 1024 * 1024),
    )(vgrad, refine_step, mix_step, tot_b)
    vgrad = vgrad.transpose(0, 2, 1, 3).reshape(depth, rows, width)
    return (vgrad, back_step, refine_step, mix_step)


def solution(mesh):
    in_specs = (
        P("gz", "xy", None),
        P(),
        P(),
        P(),
        P("gz", "xy", None, None, None, None, None),
        P("gz", "xy", None, None),
        P("gz", None, None),
    )
    out_specs = (P("gz", "xy", None), P(), P(), P())
    return jax.shard_map(body, mesh=mesh, in_specs=in_specs, out_specs=out_specs, check_vma=False)
```

```python
import functools

import jax
import jax.numpy as jnp
from jax import lax
from jax.experimental import pallas as pl
from jax.experimental.pallas import tpu as pltpu
from jax.sharding import PartitionSpec as P

EPSILON = 1e-06
F32 = jnp.float32
BF16 = jnp.bfloat16
VMEM = pl.BlockSpec(memory_space=pltpu.VMEM)
ANY = pl.BlockSpec(memory_space=pl.ANY)
HBM = pl.BlockSpec(memory_space=pltpu.HBM)
MESH = pl.DeviceIdType.MESH


def neighbours():
    return [(dz, dy) for dz in (-1, 0, 1) for dy in (-1, 0, 1) if (dz, dy) != (0, 0)]


def near(step, size):
    if step == 0:
        return pl.ds(1, size)
    return pl.ds(size, 1) if step > 0 else pl.ds(1, 1)


def far(step, size):
    if step == 0:
        return pl.ds(1, size)
    return pl.ds(0, 1) if step > 0 else pl.ds(size + 1, 1)


class Rims:
    def __init__(self, sizes, place, framed, depth, rows, lanes, send, recv):
        self.sizes, self.place, self.framed = sizes, place, framed
        self.depth, self.rows, self.lanes = depth, rows, lanes
        self.send, self.recv = send, recv

    def there(self, dz, dy):
        (n_gz, n_xy), (gz, xy) = self.sizes, self.place
        inside = (gz + dz >= 0) & (gz + dz < n_gz) & (xy + dy >= 0) & (xy + dy < n_xy)
        return inside, (gz + dz, xy + dy)

    def copy(self, dz, dy, number):
        cells = (slice(None), pl.ds(0, self.lanes))
        return pltpu.make_async_remote_copy(
            src_ref=self.framed.at[(near(dz, self.depth), near(dy, self.rows)) + cells],
            dst_ref=self.framed.at[(far(dz, self.depth), far(dy, self.rows)) + cells],
            send_sem=self.send.at[number],
            recv_sem=self.recv.at[number],
            device_id=self.there(dz, dy)[1],
            device_id_type=MESH,
        )

    def start(self):
        for number, (dz, dy) in enumerate(neighbours()):

            @pl.when(self.there(dz, dy)[0])
            def _():
                self.copy(dz, dy, number).start()

    def wait_recv(self):
        for number, (dz, dy) in enumerate(neighbours()):

            @pl.when(self.there(-dz, -dy)[0])
            def _():
                self.copy(dz, dy, number).wait_recv()

    def wait_send(self):
        for number, (dz, dy) in enumerate(neighbours()):

            @pl.when(self.there(dz, dy)[0])
            def _():
                self.copy(dz, dy, number).wait_send()


class Plane:
    def __init__(self, n_gz, n_xy, n_x, n_core):
        gz, xy = lax.axis_index("gz"), lax.axis_index("xy")
        self.gz, self.xy, self.n_x, self.n_core = gz, xy, n_x, n_core
        self.members, self.levels = n_gz * n_x, n_xy // n_x
        self.chips = self.members // n_core
        self.level, self.x = lax.div(xy, n_x), lax.rem(xy, n_x)
        self.core = lax.rem(gz, n_core)
        self.me = gz * n_x + self.x
        self.chip = lax.div(gz, n_core) * n_x + self.x

    def member(self, step):
        who = lax.rem(self.me + step, self.members)
        return who, (lax.div(who, self.n_x), self.level * self.n_x + lax.rem(who, self.n_x))

    def other_chip(self, step):
        who = lax.rem(self.chip + step, self.chips)
        gz = lax.div(who, self.n_x) * self.n_core + self.core
        return who, (gz, self.level * self.n_x + lax.rem(who, self.n_x))

    def other_core(self):
        return self.gz + 1 - 2 * self.core, self.xy

    def above(self, step):
        level = lax.rem(self.level + step, self.levels)
        return self.gz, level * self.n_x + self.x


class Total:
    def __init__(self, plane, paired, sums, mate, half_sum, got, level_got, out, send, recv):
        self.plane, self.paired, self.sums, self.mate, self.half_sum = plane, paired, sums, mate, half_sum
        self.got, self.level_got, self.out, self.send, self.recv = got, level_got, out, send, recv
        self.chunk = got.shape[1]
        self.count = plane.chips if paired else plane.members
        self.span = self.count * self.chunk
        base = plane.core * self.span if paired else 0
        self.half = pl.ds(pl.multiple_of(base, self.chunk), self.span)
        here = plane.chip if paired else plane.me
        self.mine = pl.ds(pl.multiple_of(here * self.chunk, self.chunk), self.chunk)
        self.own = pl.ds(pl.multiple_of(base + here * self.chunk, self.chunk), self.chunk)

    def peer(self, step):
        return self.plane.other_chip(step) if self.paired else self.plane.member(step)

    def remote(self, stage, source, target, device):
        return pltpu.make_async_remote_copy(
            src_ref=source,
            dst_ref=target,
            send_sem=self.send.at[stage],
            recv_sem=self.recv.at[stage],
            device_id=device,
            device_id_type=MESH,
        )

    def whole(self, stage):
        if stage in (0, 4):
            ref, device = self.mate, self.plane.other_core()
        elif stage == 2:
            ref, device = self.level_got.at[pl.ds(0, self.plane.levels - 1)], self.plane.above(1)
        else:
            ref, device = self.got, self.peer(1)[1]
        return self.remote(stage, ref, ref, device)

    def start(self):
        if self.paired:
            other = (1 - self.plane.core) * self.span
            other = pl.ds(pl.multiple_of(other, self.chunk), self.span)
            self.remote(0, self.sums.at[other], self.mate, self.plane.other_core()).start()
        else:
            self.scatter(self.sums)

    def scatter(self, source):
        for step in range(1, self.count):
            who, device = self.peer(step)
            part = pl.ds(pl.multiple_of(who * self.chunk, self.chunk), self.chunk)
            self.remote(1, source.at[part], self.got.at[step - 1], device).start()

    def pair(self):
        if self.paired:
            self.whole(0).wait_recv()
            total = self.sums[self.half, :].astype(F32) + self.mate[...].astype(F32)
            self.half_sum[...] = total.astype(BF16)
            self.scatter(self.half_sum)

    def middle(self):
        self.whole(1).wait_recv()
        total = (self.half_sum if self.paired else self.sums)[self.mine, :].astype(F32)
        for step in range(1, self.count):
            total = total + self.got[step - 1].astype(F32)
        here = self.level_got.at[self.plane.level]
        self.level_got[self.plane.level] = total.astype(BF16)
        for step in range(1, self.plane.levels):
            self.remote(2, here, here, self.plane.above(step)).start()

    def spread(self):
        self.whole(2).wait_recv()
        total = self.level_got[0].astype(F32)
        for level in range(1, self.plane.levels):
            total = total + self.level_got[level].astype(F32)
        self.out[self.own, :] = total.astype(BF16)
        here = self.out.at[self.own]
        for step in range(1, self.count):
            self.remote(3, here, here, self.peer(step)[1]).start()

    def finish(self):
        self.whole(3).wait_recv()
        if self.paired:
            here = self.out.at[self.half]
            self.remote(4, here, here, self.plane.other_core()).start()

    def end(self):
        if self.paired:
            self.whole(4).wait_recv()

    def drain(self):
        for stage in (0, 1, 2, 3, 4) if self.paired else (1, 2, 3):
            self.whole(stage).wait_send()


def weight_halves(weight, half, turned):
    lows, highs = [], []
    count = weight.shape[1] // half
    for first in range(0, count, 2):
        if first + 1 < count:
            near = weight[:, pl.ds(first * half, 2 * half)].astype(F32)
        else:
            last = weight[:, pl.ds(first * half, half)].astype(F32)
            near = jnp.concatenate([last, jnp.zeros_like(last)], axis=1)
        far = pltpu.roll(near, half, 1)
        if turned:
            both = jnp.concatenate([near, far], axis=0).T
            near, far = both[:half], both[half:]
        lows += [near, far]
        highs += [far, near]
    return lows, highs


def fill_band(target, weight, turned):
    half = weight.shape[0]
    lanes = 2 * half
    lows, highs = weight_halves(weight, half, turned)
    low = lax.broadcasted_iota(jnp.int32, (half, lanes), 1) < half
    for offset in range(9):
        ks = [26 - 3 * offset - x if turned else 3 * offset + x for x in range(3)]
        parts = [
            jnp.where(low, lows[ks[1]], highs[ks[0]]),
            jnp.where(low, lows[ks[2]], highs[ks[1]]),
            jnp.where(low, 0.0, highs[ks[2]]),
            jnp.where(low, lows[ks[0]], 0.0),
        ]
        tile = 4 * (offset // 3) + offset % 3
        for place, part in enumerate(parts):
            part = part.astype(BF16)
            target[pl.ds((4 * tile + place) * half, half), pl.ds(0, lanes)] = part
            target[pl.ds((4 * tile + 4 + place) * half, half), pl.ds(lanes, lanes)] = part
    empty = jnp.zeros((4 * half, lanes), BF16)
    for dz in range(3):
        target[pl.ds((4 * dz + 3) * 4 * half, 4 * half), pl.ds(0, lanes)] = empty
        target[pl.ds(4 * dz * 4 * half, 4 * half), pl.ds(lanes, lanes)] = empty


def side_lanes(cells, half, period):
    pairs = cells.shape[1]
    lane = lax.broadcasted_iota(jnp.int32, cells.shape, 2)
    place = lax.broadcasted_iota(jnp.int32, cells.shape, 1) % period
    right = pltpu.roll(cells, pairs - 1, 1)
    left = pltpu.roll(cells, 1, 1)
    low = lane < half
    right = jnp.where(place == period - 1, 0.0, right)
    left = jnp.where(place == 0, 0.0, left)
    return jnp.where(low, right, left)


def window_rows(windows, z, count, dz, dy):
    pairs, width = windows.shape[2], windows.shape[3]
    parts = [
        windows[pl.ds(z + dz, count), y + dy].reshape(count * pairs, width)
        for y in range(0, windows.shape[1] - 2, 2)
    ]
    return jnp.concatenate(parts, axis=0)


def conv_rows(windows, weight, z, count):
    parts = [window_rows(windows, z, count, dz, dy) for dz in range(3) for dy in range(4)]
    return jnp.dot(jnp.concatenate(parts, axis=1), weight[...], preferred_element_type=F32)


def outer_sums(out, windows, grads, half):
    depth, rows, pairs, width = windows.shape
    inner = (pl.ds(1, depth - 2), pl.ds(1, rows - 2))
    cells = (depth - 2) * (rows - 2) * pairs
    grad_turned = grads[inner + (slice(None), pl.ds(0, 2 * half))].reshape(cells, 2 * half).T
    lanes = 2 * half
    low = lax.broadcasted_iota(jnp.int32, (half, lanes), 1) < half
    held = {}

    def turn(values):
        return pltpu.roll(values, half, 1)

    for dz in range(3):
        for dy in range(3):
            seen = windows[pl.ds(dz, depth - 2), pl.ds(dy, rows - 2)].reshape(cells, width)
            both = jnp.dot(grad_turned, seen, preferred_element_type=F32)
            top_near, top_far = both[:half, :lanes], both[:half, lanes:]
            last_near, last_far = both[half:, :lanes], both[half:, lanes:]
            sums = ((top_far, last_near), (last_near, top_near), (top_near, last_far))
            for dx, (right, left) in enumerate(sums):
                k = 3 * (3 * dz + dy) + dx
                tile = 2 * (k // 4) + k % 2
                if k % 4 < 2:
                    held[tile] = turn(right) + left
                else:
                    pair = jnp.where(low, held.pop(tile), right + turn(left))
                    out[pl.ds(tile * half, half), :] = pair.astype(BF16)
    for tile, values in held.items():
        out[pl.ds(tile * half, half), :] = jnp.where(low, values, 0.0).astype(BF16)


def clear_frame(framed):
    depth, rows = framed.shape[0], framed.shape[1]
    for z in (0, depth - 1):
        framed[z] = jnp.zeros(framed.shape[1:], framed.dtype)
    side = (depth - 2, 1) + framed.shape[2:]
    for y in (0, rows - 1):
        framed[pl.ds(1, depth - 2), pl.ds(y, 1)] = jnp.zeros(side, framed.dtype)


def frame_sides(framed, half):
    depth, rows = framed.shape[0], framed.shape[1]
    pairs, lanes = framed.shape[2], 2 * half

    def fill(zs, ys):
        cells = framed[zs, ys, :, pl.ds(0, lanes)].reshape(-1, pairs, lanes).astype(F32)
        turned = side_lanes(cells, half, pairs).astype(BF16)
        framed[zs, ys, :, pl.ds(lanes, lanes)] = turned.reshape(zs.size, ys.size, pairs, lanes)

    for z in (0, depth - 1):
        fill(pl.ds(z, 1), pl.ds(0, rows))
    for y in (0, rows - 1):
        fill(pl.ds(1, depth - 2), pl.ds(y, 1))


def step_kernel(
    n_gz, n_xy, n_x, n_core, paired_a, paired_b, period,
    vol_h, cot_h, back_h, refine_h, mix_h, slot_h, count_h,
    vgrad, tot_b, refine_step, mix_step,
    vin, cin, back, refine, mix, slot, count,
    tall, cot, xw, fw, pw, gw, wb, wr, wrt, wbt, gate_s, own_s,
    tot_a, sum_a, sum_b, mate_a, mate_b, half_a, half_b, got_a, got_b, level_a, level_b,
    local, rim_send, rim_recv, grad_send, grad_recv, send_a, recv_a, send_b, recv_b,
):
    depth, pairs, rows, lanes = vin.shape
    half = lanes // 2
    slots, tiles = cin.shape[0], pairs // period
    capacity = slot.shape[0]
    step = 4 if depth % 4 == 0 else depth
    couples = rows // 2
    flat = step * couples * pairs
    block = 14 * half
    gz, xy = lax.axis_index("gz"), lax.axis_index("xy")
    place, sizes = (gz, xy), (n_gz, n_xy)
    plane = Plane(n_gz, n_xy, n_x, n_core)
    rims = Rims(sizes, place, xw, depth, rows, lanes, rim_send, rim_recv)
    grad_rims = Rims(sizes, place, gw, depth, rows, lanes, grad_send, grad_recv)
    total_a = Total(
        plane, paired_a, sum_a, mate_a, half_a, got_a, level_a, tot_a, send_a, recv_a
    )
    total_b = Total(
        plane, paired_b, sum_b, mate_b, half_b, got_b, level_b, tot_b, send_b, recv_b
    )

    loads = [
        pltpu.make_async_copy(source, target, local.at[number])
        for number, (source, target) in enumerate(
            (
                (vol_h, vin), (back_h, back), (refine_h, refine), (mix_h, mix),
                (slot_h, slot), (count_h, count), (cot_h, cin),
            )
        )
    ]
    for load in loads:
        load.start()
    for framed in (xw, gw, fw, pw):
        clear_frame(framed)

    barrier = pltpu.get_barrier_semaphore()

    def greet(device):
        pl.semaphore_signal(barrier, inc=1, device_id=device, device_id_type=MESH)

    for dz, dy in neighbours():
        inside, where = rims.there(dz, dy)

        @pl.when(inside)
        def _():
            greet(where)

    for hop in range(1, plane.members):
        greet(plane.member(hop)[1])
    for hop in range(1, plane.levels):
        greet(plane.above(hop))

    loads[0].wait()

    def turn_in(z, carry):
        tall[pl.ds(pl.multiple_of(z * pairs * rows, 8), pairs * rows), :] = (
            vin[z].astype(F32).reshape(pairs * rows, lanes)
        )
        for y in range(rows):
            cells = tall[pl.ds(z * pairs * rows + y, pairs, stride=rows), :]
            xw[z + 1, y + 1, :, pl.ds(0, lanes)] = cells.astype(BF16)
        return carry

    lax.fori_loop(0, depth, turn_in, 0)

    across = 1 + lax.min(gz, 1) + lax.min(n_gz - 1 - gz, 1)
    along = 1 + lax.min(xy, 1) + lax.min(n_xy - 1 - xy, 1)
    pl.semaphore_wait(barrier, across * along - 1 + plane.members - 1 + plane.levels - 1)
    rims.start()

    inner = pl.ds(1, rows)

    def own_sides(z, carry):
        cells = xw[z + 1, inner, :, pl.ds(0, lanes)].astype(F32)
        xw[z + 1, inner, :, pl.ds(lanes, lanes)] = side_lanes(cells, half, pairs).astype(BF16)
        return carry

    lax.fori_loop(0, depth, own_sides, 0)
    loads[1].wait()
    fill_band(wb, back, False)
    loads[2].wait()
    fill_band(wr, refine, False)
    fill_band(wrt, refine, True)
    fill_band(wbt, back, True)
    loads[3].wait()
    mixed = mix[...].astype(F32)
    mixed = jnp.concatenate([mixed, jnp.zeros_like(mixed)], axis=1)
    mix2 = jnp.concatenate([mixed, pltpu.roll(mixed, half, 1)], axis=0).T
    blank = jnp.zeros_like(mix2)
    mix4 = jnp.concatenate(
        [jnp.concatenate([mix2, blank], axis=1), jnp.concatenate([blank, mix2], axis=1)], axis=0
    ).astype(BF16)

    for load in loads[4:]:
        load.wait()
    picks = []
    for number in range(slots):
        owner, place_in = number // capacity, number % capacity
        live = place_in < count[xy, owner]
        which = slot[place_in, owner]
        picks.append([jnp.where(live & (which == tile), 1.0, 0.0) for tile in range(tiles)])

    def pick(z, carry):
        held = [None] * tiles
        for number in range(slots):
            cells = cin[number, z].astype(F32)
            for tile in range(tiles):
                term = cells * picks[number][tile]
                held[tile] = term if held[tile] is None else held[tile] + term
        span = period * rows
        for tile in range(tiles):
            start = pl.multiple_of(z * pairs * rows + tile * span, 8)
            tall[pl.ds(start, span), :] = held[tile].reshape(span, lanes)
        for y in range(rows):
            cot[lax.div(z, step), y // 2, lax.rem(z, step), :, pl.ds(y % 2 * lanes, lanes)] = tall[
                pl.ds(z * pairs * rows + y, pairs, stride=rows), :
            ]
        return carry

    lax.fori_loop(0, depth, pick, 0)

    rims.wait_recv()
    frame_sides(xw, half)

    def put(target, z, cells, period):
        for y in range(rows):
            odd, first = y % 2, y // 2 * step * pairs
            own = cells[first : first + step * pairs, odd * lanes : (odd + 1) * lanes]
            own = own.reshape(step, pairs, lanes)
            target[pl.ds(z + 1, step), y + 1, :, pl.ds(0, lanes)] = own
            target[pl.ds(z + 1, step), y + 1, :, pl.ds(lanes, lanes)] = side_lanes(
                own.astype(F32), half, period
            ).astype(BF16)

    def take(framed, z):
        parts = [framed[pl.ds(z + 1, step), y + 1, :, pl.ds(0, lanes)] for y in range(rows)]
        parts = [part.reshape(step * pairs, lanes) for part in parts]
        lines = [jnp.concatenate(parts[odd::2], axis=0) for odd in range(2)]
        return jnp.concatenate(lines, axis=1).astype(F32)

    def line(z):
        return pl.ds(z * couples * pairs, flat)

    for z in range(0, depth, step):
        put(fw, z, (take(xw, z) + conv_rows(xw, wb, z, step)).astype(BF16), period)
    for z in range(0, depth, step):
        pre = conv_rows(fw, wr, z, step)
        sig = jax.nn.sigmoid(pre)
        upstream = cot[z // step].reshape(flat, 2 * lanes).astype(BF16)
        gate_s[line(z), :] = (pre * sig).astype(BF16)
        gated_grad = jnp.dot(upstream, mix4, preferred_element_type=F32)
        pre_grad = (gated_grad * sig * (1.0 + pre * (1.0 - sig))).astype(BF16)
        put(pw, z, pre_grad, period)

    outer_sums(sum_a, fw, pw, half)
    cot_rows = cot[...].reshape(depth * couples * pairs, 2 * lanes).astype(BF16)
    both = jnp.dot(gate_s[...].T, cot_rows, preferred_element_type=F32)
    both = both[:lanes, :lanes] + both[lanes:, lanes:]
    lane = lax.broadcasted_iota(jnp.int32, (half, lanes), 1)
    sum_a[pl.ds(block, half), :] = jnp.where(
        lane < half, both[:half] + pltpu.roll(both[half:], half, 1), 0.0
    ).astype(BF16)
    used = block + half
    if used < sum_a.shape[0]:
        sum_a[pl.ds(used, sum_a.shape[0] - used), :] = jnp.zeros((sum_a.shape[0] - used, lanes), BF16)
    total_a.start()

    for z in range(0, depth, step):
        upstream = cot[z // step].reshape(flat, 2 * lanes)
        grad = (upstream + conv_rows(pw, wrt, z, step)).astype(BF16)
        own_s[line(z), :] = grad
        put(gw, z, grad, pairs)
    grad_rims.start()
    total_a.pair()

    outer_sums(sum_b, xw, gw, half)
    if block < sum_b.shape[0]:
        sum_b[pl.ds(block, sum_b.shape[0] - block), :] = jnp.zeros((sum_b.shape[0] - block, lanes), BF16)
    total_b.start()
    total_b.pair()
    total_a.middle()

    grad_rims.wait_recv()
    frame_sides(gw, half)

    def back_conv(z):
        grad = own_s[line(z), :].astype(F32) + conv_rows(gw, wbt, z, step)
        grad = grad.reshape(couples, step, pairs, 2 * lanes)
        for y in range(rows):
            for level in range(step):
                tall[pl.ds(((z + level) * rows + y) * pairs, pairs), :] = grad[
                    y // 2, level, :, y % 2 * lanes : (y % 2 + 1) * lanes
                ]

    back_conv(0)
    total_b.middle()
    for z in range(step, depth, step):
        back_conv(z)
    total_a.spread()

    def turn_out(z, carry):
        for pair in range(pairs):
            cells = tall[pl.ds(z * pairs * rows + pair, rows, stride=pairs), :]
            vgrad[z, pair] = cells.astype(BF16)
        return carry

    lax.fori_loop(0, depth, turn_out, 0)
    total_b.spread()
    total_a.finish()
    total_a.end()
    write_step(tot_a, refine_step, half)
    values = tot_a[pl.ds(block, half), :].astype(F32)
    mix_step[...] = (values / scale_of(values, 1.0 * half * half))[:, :half]
    total_b.finish()
    total_b.end()
    rims.wait_send()
    grad_rims.wait_send()
    total_a.drain()
    total_b.drain()


def scale_of(values, count):
    squares = jnp.sum(values * values, axis=0, keepdims=True)
    return jnp.sqrt(jnp.sum(squares, axis=1, keepdims=True) / count + EPSILON)


def write_step(totals, out, half):
    lanes = 2 * half
    values = totals[pl.ds(0, 14 * half), :].astype(F32)
    scale = scale_of(values, 27.0 * half * half)
    for quad in range(7):
        turned = values[quad * lanes : (quad + 1) * lanes].T / scale
        out[:, pl.ds(quad * 2 * lanes, lanes)] = turned[:half]
        wide = min(lanes, out.shape[1] - quad * 2 * lanes - lanes)
        out[:, pl.ds(quad * 2 * lanes + lanes, wide)] = turned[half:, :wide]


def finish_kernel(
    vgrad, refine_step, mix_step, tot_b, vgrad_out, back_out, refine_out, mix_out, back_step, sems
):
    copies = [
        pltpu.make_async_copy(source, target, sems.at[number])
        for number, (source, target) in enumerate(
            ((vgrad, vgrad_out), (refine_step, refine_out), (mix_step, mix_out), (back_step, back_out))
        )
    ]
    for copy in copies[:3]:
        copy.start()
    write_step(tot_b, back_step, mix_step.shape[0])
    copies[3].start()
    for copy in copies:
        copy.wait()


def body(volume, backbone_weight, refine_weight, mix_weight, tile_cot, tile_slot, tile_count):
    depth, rows, width = volume.shape
    channels = mix_weight.shape[0]
    edge = tile_cot.shape[4]
    owners, capacity = tile_cot.shape[2], tile_cot.shape[3]
    assert depth == edge and rows == edge and rows % 2 == 0
    lanes = 2 * channels
    pairs = width // lanes
    period = edge // 2
    slots = owners * capacity
    n_gz, n_xy = lax.axis_size("gz"), lax.axis_size("xy")
    n_x = max(n_gz // 2, 1)
    if n_xy % n_x:
        n_x = 1
    members, levels = n_gz * n_x, n_xy // n_x
    n_core = 2 if n_gz % 2 == 0 else 1
    paired_a, paired_b = n_core == 2 and True, n_core == 2 and False
    count_a = members // 2 if paired_a else members
    count_b = members // 2 if paired_b else members

    vol = volume.reshape(depth, rows, pairs, lanes).transpose(0, 2, 1, 3)
    cot = tile_cot.reshape(slots, edge, edge, period, lanes).transpose(0, 1, 3, 2, 4)
    slot = tile_slot.reshape(owners, capacity).T
    count = tile_count.reshape(owners, owners)

    block = 14 * channels
    chunk_a = -(-(block + channels) // (members * 16)) * 16
    chunk_b = -(-block // (members * 16)) * 16
    framed = pltpu.VMEM((depth + 2, rows + 2, pairs, 2 * lanes), BF16)
    band = pltpu.VMEM((48 * channels, 2 * lanes), BF16)
    wide = jax.ShapeDtypeStruct((channels, 27 * channels), F32)
    small = jax.ShapeDtypeStruct((channels, channels), F32)
    cells = depth * rows * pairs
    dma = pltpu.SemaphoreType.DMA
    step = 4 if depth % 4 == 0 else depth
    operands = (vol, cot, backbone_weight, refine_weight, mix_weight, slot, count)
    vgrad, tot_b, refine_step, mix_step = pl.pallas_call(
        functools.partial(step_kernel, n_gz, n_xy, n_x, n_core, paired_a, paired_b, period),
        out_shape=(
            jax.ShapeDtypeStruct(vol.shape, BF16),
            jax.ShapeDtypeStruct((members * chunk_b, lanes), BF16),
            wide,
            small,
        ),
        in_specs=[HBM] * 7,
        out_specs=(VMEM,) * 4,
        scratch_shapes=[
            pltpu.VMEM(vol.shape, BF16),
            pltpu.VMEM(cot.shape, BF16),
            pltpu.VMEM(backbone_weight.shape, BF16),
            pltpu.VMEM(refine_weight.shape, BF16),
            pltpu.VMEM(mix_weight.shape, BF16),
            pltpu.SMEM(slot.shape, jnp.int32),
            pltpu.SMEM(count.shape, jnp.int32),
            pltpu.VMEM((cells, lanes), F32),
            pltpu.VMEM((depth // step, rows // 2, step, pairs, 2 * lanes), F32),
            framed, framed, framed, framed,
            band, band, band, band,
            pltpu.VMEM((cells // 2, 2 * lanes), BF16),
            pltpu.VMEM((cells // 2, 2 * lanes), BF16),
            pltpu.VMEM((members * chunk_a, lanes), BF16),
            pltpu.VMEM((members * chunk_a, lanes), BF16),
            pltpu.VMEM((members * chunk_b, lanes), BF16),
            pltpu.VMEM((count_a * chunk_a, lanes), BF16),
            pltpu.VMEM((count_b * chunk_b, lanes), BF16),
            pltpu.VMEM((count_a * chunk_a, lanes), BF16),
            pltpu.VMEM((count_b * chunk_b, lanes), BF16),
            pltpu.VMEM((count_a - 1, chunk_a, lanes), BF16),
            pltpu.VMEM((count_b - 1, chunk_b, lanes), BF16),
            pltpu.VMEM((levels, chunk_a, lanes), BF16),
            pltpu.VMEM((levels, chunk_b, lanes), BF16),
            dma((7,)),
            dma((8,)), dma((8,)), dma((8,)), dma((8,)),
            dma((5,)), dma((5,)), dma((5,)), dma((5,)),
        ],
        compiler_params=pltpu.CompilerParams(
            collective_id=0, has_side_effects=True, vmem_limit_bytes=32 * 1024 * 1024
        ),
    )(*[pltpu.with_memory_space_constraint(operand, pltpu.HBM) for operand in operands])
    vgrad, back_step, refine_step, mix_step = pl.pallas_call(
        finish_kernel,
        out_shape=(jax.ShapeDtypeStruct(vol.shape, BF16), wide, wide, small),
        in_specs=[VMEM] * 4,
        out_specs=(ANY,) * 4,
        scratch_shapes=[pltpu.VMEM(wide.shape, F32), dma((4,))],
        compiler_params=pltpu.CompilerParams(vmem_limit_bytes=8 * 1024 * 1024),
    )(vgrad, refine_step, mix_step, tot_b)
    vgrad = vgrad.transpose(0, 2, 1, 3).reshape(depth, rows, width)
    return (vgrad, back_step, refine_step, mix_step)


def solution(mesh):
    in_specs = (
        P("gz", "xy", None),
        P(),
        P(),
        P(),
        P("gz", "xy", None, None, None, None, None),
        P("gz", "xy", None, None),
        P("gz", None, None),
    )
    out_specs = (P("gz", "xy", None), P(), P(), P())
    return jax.shard_map(body, mesh=mesh, in_specs=in_specs, out_specs=out_specs, check_vma=False)
```

```python
import functools

import jax
import jax.numpy as jnp
from jax import lax
from jax.experimental import pallas as pl
from jax.experimental.pallas import tpu as pltpu
from jax.sharding import PartitionSpec as P

EPSILON = 1e-06
F32 = jnp.float32
BF16 = jnp.bfloat16
VMEM = pl.BlockSpec(memory_space=pltpu.VMEM)
ANY = pl.BlockSpec(memory_space=pl.ANY)
HBM = pl.BlockSpec(memory_space=pltpu.HBM)
MESH = pl.DeviceIdType.MESH


def neighbours():
    return [(dz, dy) for dz in (-1, 0, 1) for dy in (-1, 0, 1) if (dz, dy) != (0, 0)]


def near(step, size):
    if step == 0:
        return pl.ds(1, size)
    return pl.ds(size, 1) if step > 0 else pl.ds(1, 1)


def far(step, size):
    if step == 0:
        return pl.ds(1, size)
    return pl.ds(0, 1) if step > 0 else pl.ds(size + 1, 1)


class Rims:
    def __init__(self, sizes, place, framed, depth, rows, lanes, send, recv):
        self.sizes, self.place, self.framed = sizes, place, framed
        self.depth, self.rows, self.lanes = depth, rows, lanes
        self.send, self.recv = send, recv

    def there(self, dz, dy):
        (n_gz, n_xy), (gz, xy) = self.sizes, self.place
        inside = (gz + dz >= 0) & (gz + dz < n_gz) & (xy + dy >= 0) & (xy + dy < n_xy)
        return inside, (gz + dz, xy + dy)

    def copy(self, dz, dy, number):
        cells = (slice(None), pl.ds(0, self.lanes))
        return pltpu.make_async_remote_copy(
            src_ref=self.framed.at[(near(dz, self.depth), near(dy, self.rows)) + cells],
            dst_ref=self.framed.at[(far(dz, self.depth), far(dy, self.rows)) + cells],
            send_sem=self.send.at[number],
            recv_sem=self.recv.at[number],
            device_id=self.there(dz, dy)[1],
            device_id_type=MESH,
        )

    def start(self):
        for number, (dz, dy) in enumerate(neighbours()):

            @pl.when(self.there(dz, dy)[0])
            def _():
                self.copy(dz, dy, number).start()

    def wait_recv(self):
        for number, (dz, dy) in enumerate(neighbours()):

            @pl.when(self.there(-dz, -dy)[0])
            def _():
                self.copy(dz, dy, number).wait_recv()

    def wait_send(self):
        for number, (dz, dy) in enumerate(neighbours()):

            @pl.when(self.there(dz, dy)[0])
            def _():
                self.copy(dz, dy, number).wait_send()


class Plane:
    def __init__(self, n_gz, n_xy, n_x, n_core):
        gz, xy = lax.axis_index("gz"), lax.axis_index("xy")
        self.gz, self.xy, self.n_x, self.n_core = gz, xy, n_x, n_core
        self.members, self.levels = n_gz * n_x, n_xy // n_x
        self.chips = self.members // n_core
        self.level, self.x = lax.div(xy, n_x), lax.rem(xy, n_x)
        self.core = lax.rem(gz, n_core)
        self.chip = lax.div(gz, n_core) * n_x + self.x
        self.me = self.core * self.chips + self.chip

    def member(self, step):
        who = lax.rem(self.me + step, self.members)
        core, chip = lax.div(who, self.chips), lax.rem(who, self.chips)
        gz = lax.div(chip, self.n_x) * self.n_core + core
        return who, (gz, self.level * self.n_x + lax.rem(chip, self.n_x))

    def other_chip(self, step):
        who = lax.rem(self.chip + step, self.chips)
        gz = lax.div(who, self.n_x) * self.n_core + self.core
        return who, (gz, self.level * self.n_x + lax.rem(who, self.n_x))

    def other_core(self):
        return self.gz + 1 - 2 * self.core, self.xy

    def above(self, step):
        level = lax.rem(self.level + step, self.levels)
        return self.gz, level * self.n_x + self.x


class Total:
    def __init__(self, plane, paired, joined, out, sums, mate, half_sum, got, level_got, send, recv):
        self.joined = joined
        self.plane, self.paired, self.sums, self.mate, self.half_sum = plane, paired, sums, mate, half_sum
        self.got, self.level_got, self.out, self.send, self.recv = got, level_got, out, send, recv
        self.chunk = got.shape[1]
        self.count = plane.chips if paired else plane.members
        self.span = self.count * self.chunk
        base = plane.core * plane.chips * self.chunk
        self.half = pl.ds(pl.multiple_of(base, self.chunk), plane.chips * self.chunk)
        here = plane.chip if paired else plane.me
        self.mine = pl.ds(pl.multiple_of(here * self.chunk, self.chunk), self.chunk)
        self.own = pl.ds(pl.multiple_of(plane.me * self.chunk, self.chunk), self.chunk)
        self.readers = plane.chips if joined else plane.members

    def peer(self, step):
        return self.plane.other_chip(step) if self.paired else self.plane.member(step)

    def remote(self, stage, source, target, device):
        return pltpu.make_async_remote_copy(
            src_ref=source,
            dst_ref=target,
            send_sem=self.send.at[stage],
            recv_sem=self.recv.at[stage],
            device_id=device,
            device_id_type=MESH,
        )

    def whole(self, stage):
        if stage == 0:
            ref, device = self.mate, self.plane.other_core()
        elif stage == 4:
            ref, device = self.out.at[self.half], self.plane.other_core()
        elif stage == 3:
            ref = self.out.at[pl.ds(0, (self.readers - 1) * self.chunk)]
            device = self.plane.member(1)[1]
        elif stage == 2:
            ref, device = self.level_got.at[pl.ds(0, self.plane.levels - 1)], self.plane.above(1)
        else:
            ref, device = self.got, self.peer(1)[1]
        return self.remote(stage, ref, ref, device)

    def start(self):
        if self.paired:
            other = (1 - self.plane.core) * self.span
            other = pl.ds(pl.multiple_of(other, self.chunk), self.span)
            self.remote(0, self.sums.at[other], self.mate, self.plane.other_core()).start()
        else:
            self.scatter(self.sums)

    def scatter(self, source):
        for step in range(1, self.count):
            who, device = self.peer(step)
            part = pl.ds(pl.multiple_of(who * self.chunk, self.chunk), self.chunk)
            self.remote(1, source.at[part], self.got.at[step - 1], device).start()

    def pair(self):
        if self.paired:
            self.whole(0).wait_recv()
            total = self.sums[self.half, :].astype(F32) + self.mate[...].astype(F32)
            self.half_sum[...] = total.astype(BF16)
            self.scatter(self.half_sum)

    def middle(self):
        self.whole(1).wait_recv()
        total = (self.half_sum if self.paired else self.sums)[self.mine, :].astype(F32)
        for step in range(1, self.count):
            total = total + self.got[step - 1].astype(F32)
        here = self.level_got.at[self.plane.level]
        self.level_got[self.plane.level] = total.astype(BF16)
        for step in range(1, self.plane.levels):
            self.remote(2, here, here, self.plane.above(step)).start()

    def spread(self):
        self.whole(2).wait_recv()
        total = self.level_got[0].astype(F32)
        for level in range(1, self.plane.levels):
            total = total + self.level_got[level].astype(F32)
        self.out[self.own, :] = total.astype(BF16)
        here = self.out.at[self.own]
        for step in range(1, self.readers):
            reader = self.plane.other_chip(step) if self.joined else self.plane.member(step)
            self.remote(3, here, here, reader[1]).start()

    def finish(self):
        self.whole(3).wait_recv()
        if self.joined:
            here = self.out.at[self.half]
            self.remote(4, here, here, self.plane.other_core()).start()

    def end(self):
        if self.joined:
            self.whole(4).wait_recv()

    def drain(self):
        for stage in [0] * self.paired + [1, 2, 3] + [4] * self.joined:
            self.whole(stage).wait_send()


def weight_halves(weight, half, turned):
    lows, highs = [], []
    count = weight.shape[1] // half
    for first in range(0, count, 2):
        if first + 1 < count:
            near = weight[:, pl.ds(first * half, 2 * half)].astype(F32)
        else:
            last = weight[:, pl.ds(first * half, half)].astype(F32)
            near = jnp.concatenate([last, jnp.zeros_like(last)], axis=1)
        far = pltpu.roll(near, half, 1)
        if turned:
            both = jnp.concatenate([near, far], axis=0).T
            near, far = both[:half], both[half:]
        lows += [near, far]
        highs += [far, near]
    return lows, highs


def fill_band(target, weight, turned):
    half = weight.shape[0]
    lanes = 2 * half
    lows, highs = weight_halves(weight, half, turned)
    low = lax.broadcasted_iota(jnp.int32, (half, lanes), 1) < half
    for offset in range(9):
        ks = [26 - 3 * offset - x if turned else 3 * offset + x for x in range(3)]
        parts = [
            jnp.where(low, lows[ks[1]], highs[ks[0]]),
            jnp.where(low, lows[ks[2]], highs[ks[1]]),
            jnp.where(low, 0.0, highs[ks[2]]),
            jnp.where(low, lows[ks[0]], 0.0),
        ]
        tile = 4 * (offset // 3) + offset % 3
        for place, part in enumerate(parts):
            part = part.astype(BF16)
            target[pl.ds((4 * tile + place) * half, half), pl.ds(0, lanes)] = part
            target[pl.ds((4 * tile + 4 + place) * half, half), pl.ds(lanes, lanes)] = part
    empty = jnp.zeros((4 * half, lanes), BF16)
    for dz in range(3):
        target[pl.ds((4 * dz + 3) * 4 * half, 4 * half), pl.ds(0, lanes)] = empty
        target[pl.ds(4 * dz * 4 * half, 4 * half), pl.ds(lanes, lanes)] = empty


def side_lanes(cells, half, period):
    pairs = cells.shape[1]
    lane = lax.broadcasted_iota(jnp.int32, cells.shape, 2)
    place = lax.broadcasted_iota(jnp.int32, cells.shape, 1) % period
    right = pltpu.roll(cells, pairs - 1, 1)
    left = pltpu.roll(cells, 1, 1)
    low = lane < half
    right = jnp.where(place == period - 1, 0.0, right)
    left = jnp.where(place == 0, 0.0, left)
    return jnp.where(low, right, left)


def window_rows(windows, z, count, dz, dy):
    pairs, width = windows.shape[2], windows.shape[3]
    parts = [
        windows[pl.ds(z + dz, count), y + dy].reshape(count * pairs, width)
        for y in range(0, windows.shape[1] - 2, 2)
    ]
    return jnp.concatenate(parts, axis=0)


def conv_rows(windows, weight, z, count):
    parts = [window_rows(windows, z, count, dz, dy) for dz in range(3) for dy in range(4)]
    return jnp.dot(jnp.concatenate(parts, axis=1), weight[...], preferred_element_type=F32)


def outer_sums(parts, split, hook, windows, grads, half):
    depth, rows, pairs, width = windows.shape
    inner = (pl.ds(1, depth - 2), pl.ds(1, rows - 2))
    cells = (depth - 2) * (rows - 2) * pairs
    grad_turned = grads[inner + (slice(None), pl.ds(0, 2 * half))].reshape(cells, 2 * half).T
    lanes = 2 * half
    low = lax.broadcasted_iota(jnp.int32, (half, lanes), 1) < half
    held = {}

    def put(tile, values):
        part, first = (parts[0], 0) if tile < split else (parts[1], split)
        part[pl.ds((tile - first) * half, half), :] = values.astype(BF16)

    def turn(values):
        return pltpu.roll(values, half, 1)

    for dz in range(3):
        for dy in range(3):
            seen = windows[pl.ds(dz, depth - 2), pl.ds(dy, rows - 2)].reshape(cells, width)
            both = jnp.dot(grad_turned, seen, preferred_element_type=F32)
            top_near, top_far = both[:half, :lanes], both[:half, lanes:]
            last_near, last_far = both[half:, :lanes], both[half:, lanes:]
            sums = ((top_far, last_near), (last_near, top_near), (top_near, last_far))
            for dx, (right, left) in enumerate(sums):
                k = 3 * (3 * dz + dy) + dx
                tile = 2 * (k // 4) + k % 2
                if k % 4 < 2:
                    held[tile] = turn(right) + left
                else:
                    pair = jnp.where(low, held.pop(tile), right + turn(left))
                    put(tile, pair)
                    if tile == split - 1:
                        hook()
    for tile, values in held.items():
        put(tile, jnp.where(low, values, 0.0))


def clear_frame(framed):
    depth, rows = framed.shape[0], framed.shape[1]
    for z in (0, depth - 1):
        framed[z] = jnp.zeros(framed.shape[1:], framed.dtype)
    side = (depth - 2, 1) + framed.shape[2:]
    for y in (0, rows - 1):
        framed[pl.ds(1, depth - 2), pl.ds(y, 1)] = jnp.zeros(side, framed.dtype)


def frame_sides(framed, half):
    depth, rows = framed.shape[0], framed.shape[1]
    pairs, lanes = framed.shape[2], 2 * half

    def fill(zs, ys):
        cells = framed[zs, ys, :, pl.ds(0, lanes)].reshape(-1, pairs, lanes).astype(F32)
        turned = side_lanes(cells, half, pairs).astype(BF16)
        framed[zs, ys, :, pl.ds(lanes, lanes)] = turned.reshape(zs.size, ys.size, pairs, lanes)

    for z in (0, depth - 1):
        fill(pl.ds(z, 1), pl.ds(0, rows))
    for y in (0, rows - 1):
        fill(pl.ds(1, depth - 2), pl.ds(y, 1))


def step_kernel(
    n_gz, n_xy, n_x, n_core, paired, joined, period,
    vol_h, cot_h, back_h, refine_h, mix_h, slot_h, count_h,
    vgrad, tot_2, tot_3, refine_step, mix_step,
    vin, cin, back, refine, mix, slot, count,
    tall, cot, xw, fw, pw, gw, wb, wr, wrt, wbt, gate_s, own_s,
    tot_0, tot_1,
    local, rim_send, rim_recv, grad_recv, *pieces,
):
    depth, pairs, rows, lanes = vin.shape
    half = lanes // 2
    slots, tiles = cin.shape[0], pairs // period
    capacity = slot.shape[0]
    step = 4 if depth % 4 == 0 else depth
    couples = rows // 2
    flat = step * couples * pairs
    split = 8
    gz, xy = lax.axis_index("gz"), lax.axis_index("xy")
    place, sizes = (gz, xy), (n_gz, n_xy)
    plane = Plane(n_gz, n_xy, n_x, n_core)
    rims = Rims(sizes, place, xw, depth, rows, lanes, rim_send, rim_recv)
    grad_rims = Rims(sizes, place, gw, depth, rows, lanes, rim_send, grad_recv)
    totals = []
    for number, tot in enumerate((tot_0, tot_1, tot_2, tot_3)):
        totals.append(Total(plane, paired[number], joined[number], tot, *pieces[7 * number : 7 * number + 7]))

    loads = [
        pltpu.make_async_copy(source, target, local.at[number])
        for number, (source, target) in enumerate(
            (
                (vol_h, vin), (back_h, back), (refine_h, refine), (mix_h, mix),
                (slot_h, slot), (count_h, count), (cot_h, cin),
            )
        )
    ]
    for load in loads:
        load.start()
    for framed in (xw, gw, fw, pw):
        clear_frame(framed)

    barrier = pltpu.get_barrier_semaphore()

    def greet(device):
        pl.semaphore_signal(barrier, inc=1, device_id=device, device_id_type=MESH)

    for dz, dy in neighbours():
        inside, where = rims.there(dz, dy)

        @pl.when(inside)
        def _():
            greet(where)

    for hop in range(1, plane.members):
        greet(plane.member(hop)[1])
    for hop in range(1, plane.levels):
        greet(plane.above(hop))

    loads[0].wait()

    def turn_in(z, carry):
        tall[pl.ds(pl.multiple_of(z * pairs * rows, 8), pairs * rows), :] = (
            vin[z].astype(F32).reshape(pairs * rows, lanes)
        )
        for y in range(rows):
            cells = tall[pl.ds(z * pairs * rows + y, pairs, stride=rows), :]
            xw[z + 1, y + 1, :, pl.ds(0, lanes)] = cells.astype(BF16)
        return carry

    lax.fori_loop(0, depth, turn_in, 0)

    across = 1 + lax.min(gz, 1) + lax.min(n_gz - 1 - gz, 1)
    along = 1 + lax.min(xy, 1) + lax.min(n_xy - 1 - xy, 1)
    pl.semaphore_wait(barrier, across * along - 1 + plane.members - 1 + plane.levels - 1)
    rims.start()

    inner = pl.ds(1, rows)

    def own_sides(z, carry):
        cells = xw[z + 1, inner, :, pl.ds(0, lanes)].astype(F32)
        xw[z + 1, inner, :, pl.ds(lanes, lanes)] = side_lanes(cells, half, pairs).astype(BF16)
        return carry

    lax.fori_loop(0, depth, own_sides, 0)
    loads[1].wait()
    fill_band(wb, back, False)
    loads[2].wait()
    fill_band(wr, refine, False)
    fill_band(wrt, refine, True)
    fill_band(wbt, back, True)
    loads[3].wait()
    mixed = mix[...].astype(F32)
    mixed = jnp.concatenate([mixed, jnp.zeros_like(mixed)], axis=1)
    mix2 = jnp.concatenate([mixed, pltpu.roll(mixed, half, 1)], axis=0).T
    blank = jnp.zeros_like(mix2)
    mix4 = jnp.concatenate(
        [jnp.concatenate([mix2, blank], axis=1), jnp.concatenate([blank, mix2], axis=1)], axis=0
    ).astype(BF16)

    for load in loads[4:]:
        load.wait()
    picks = []
    for number in range(slots):
        owner, place_in = number // capacity, number % capacity
        live = place_in < count[xy, owner]
        which = slot[place_in, owner]
        picks.append([jnp.where(live & (which == tile), 1.0, 0.0) for tile in range(tiles)])

    def pick(z, carry):
        held = [None] * tiles
        for number in range(slots):
            cells = cin[number, z].astype(F32)
            for tile in range(tiles):
                term = cells * picks[number][tile]
                held[tile] = term if held[tile] is None else held[tile] + term
        span = period * rows
        for tile in range(tiles):
            start = pl.multiple_of(z * pairs * rows + tile * span, 8)
            tall[pl.ds(start, span), :] = held[tile].reshape(span, lanes)
        for y in range(rows):
            cot[lax.div(z, step), y // 2, lax.rem(z, step), :, pl.ds(y % 2 * lanes, lanes)] = tall[
                pl.ds(z * pairs * rows + y, pairs, stride=rows), :
            ]
        return carry

    lax.fori_loop(0, depth, pick, 0)

    rims.wait_recv()
    frame_sides(xw, half)

    def put(target, z, cells, period):
        for y in range(rows):
            odd, first = y % 2, y // 2 * step * pairs
            own = cells[first : first + step * pairs, odd * lanes : (odd + 1) * lanes]
            own = own.reshape(step, pairs, lanes)
            target[pl.ds(z + 1, step), y + 1, :, pl.ds(0, lanes)] = own
            target[pl.ds(z + 1, step), y + 1, :, pl.ds(lanes, lanes)] = side_lanes(
                own.astype(F32), half, period
            ).astype(BF16)

    def take(framed, z):
        parts = [framed[pl.ds(z + 1, step), y + 1, :, pl.ds(0, lanes)] for y in range(rows)]
        parts = [part.reshape(step * pairs, lanes) for part in parts]
        lines = [jnp.concatenate(parts[odd::2], axis=0) for odd in range(2)]
        return jnp.concatenate(lines, axis=1).astype(F32)

    def line(z):
        return pl.ds(z * couples * pairs, flat)

    for z in range(0, depth, step):
        put(fw, z, (take(xw, z) + conv_rows(xw, wb, z, step)).astype(BF16), period)
    for z in range(0, depth, step):
        pre = conv_rows(fw, wr, z, step)
        sig = jax.nn.sigmoid(pre)
        upstream = cot[z // step].reshape(flat, 2 * lanes).astype(BF16)
        gate_s[line(z), :] = (pre * sig).astype(BF16)
        gated_grad = jnp.dot(upstream, mix4, preferred_element_type=F32)
        pre_grad = (gated_grad * sig * (1.0 + pre * (1.0 - sig))).astype(BF16)
        put(pw, z, pre_grad, period)

    def begin(number):
        part = totals[number].sums
        used = (split if number % 2 == 0 else 15 - split if number == 1 else 14 - split) * half
        if used < part.shape[0]:
            part[pl.ds(used, part.shape[0] - used), :] = jnp.zeros((part.shape[0] - used, lanes), BF16)
        totals[number].start()

    outer_sums((totals[0].sums, totals[1].sums), split, lambda: begin(0), fw, pw, half)
    cot_rows = cot[...].reshape(depth * couples * pairs, 2 * lanes).astype(BF16)
    both = jnp.dot(gate_s[...].T, cot_rows, preferred_element_type=F32)
    both = both[:lanes, :lanes] + both[lanes:, lanes:]
    lane = lax.broadcasted_iota(jnp.int32, (half, lanes), 1)
    totals[1].sums[pl.ds((14 - split) * half, half), :] = jnp.where(
        lane < half, both[:half] + pltpu.roll(both[half:], half, 1), 0.0
    ).astype(BF16)
    begin(1)

    for z in range(0, depth, step):
        upstream = cot[z // step].reshape(flat, 2 * lanes)
        grad = (upstream + conv_rows(pw, wrt, z, step)).astype(BF16)
        own_s[line(z), :] = grad
        put(gw, z, grad, pairs)
    for total in totals[:2]:
        total.pair()

    outer_sums((totals[2].sums, totals[3].sums), split, lambda: begin(2), xw, gw, half)
    begin(3)
    rims.wait_send()
    grad_rims.start()
    for total in totals[2:]:
        total.pair()
    for total in totals[:2]:
        total.middle()
    for total in totals[2:]:
        total.middle()

    grad_rims.wait_recv()
    frame_sides(gw, half)

    def back_conv(z):
        grad = own_s[line(z), :].astype(F32) + conv_rows(gw, wbt, z, step)
        grad = grad.reshape(couples, step, pairs, 2 * lanes)
        for y in range(rows):
            for level in range(step):
                tall[pl.ds(((z + level) * rows + y) * pairs, pairs), :] = grad[
                    y // 2, level, :, y % 2 * lanes : (y % 2 + 1) * lanes
                ]

    back_conv(0)
    for total in totals[:2]:
        total.spread()
    for z in range(step, depth, step):
        back_conv(z)

    def turn_out(z, carry):
        for pair in range(pairs):
            cells = tall[pl.ds(z * pairs * rows + pair, rows, stride=pairs), :]
            vgrad[z, pair] = cells.astype(BF16)
        return carry

    lax.fori_loop(0, depth, turn_out, 0)
    for total in totals[2:]:
        total.spread()
    for total in totals[:2]:
        total.finish()
    for total in totals[:2]:
        total.end()
    write_step(tot_0, tot_1, split, refine_step, half)
    values = tot_1[pl.ds((14 - split) * half, half), :].astype(F32)
    mix_step[...] = (values / scale_of(values, 1.0 * half * half))[:, :half]
    for total in totals[2:]:
        total.finish()
    for total in totals[2:]:
        total.end()
    grad_rims.wait_send()
    for total in totals:
        total.drain()


def scale_of(values, count):
    squares = jnp.sum(values * values, axis=0, keepdims=True)
    return jnp.sqrt(jnp.sum(squares, axis=1, keepdims=True) / count + EPSILON)


def write_step(first, second, split, out, half):
    lanes = 2 * half
    values = jnp.concatenate(
        [first[pl.ds(0, split * half), :], second[pl.ds(0, (14 - split) * half), :]], axis=0
    ).astype(F32)
    scale = scale_of(values, 27.0 * half * half)
    for quad in range(7):
        turned = values[quad * lanes : (quad + 1) * lanes].T / scale
        out[:, pl.ds(quad * 2 * lanes, lanes)] = turned[:half]
        wide = min(lanes, out.shape[1] - quad * 2 * lanes - lanes)
        out[:, pl.ds(quad * 2 * lanes + lanes, wide)] = turned[half:, :wide]


def finish_kernel(
    vgrad, refine_step, mix_step, tot_2, tot_3, vgrad_out, back_out, refine_out, mix_out, back_step, sems
):
    copies = [
        pltpu.make_async_copy(source, target, sems.at[number])
        for number, (source, target) in enumerate(
            ((vgrad, vgrad_out), (refine_step, refine_out), (mix_step, mix_out), (back_step, back_out))
        )
    ]
    for copy in copies[:3]:
        copy.start()
    write_step(tot_2, tot_3, 8, back_step, mix_step.shape[0])
    copies[3].start()
    for copy in copies:
        copy.wait()


def body(volume, backbone_weight, refine_weight, mix_weight, tile_cot, tile_slot, tile_count):
    depth, rows, width = volume.shape
    channels = mix_weight.shape[0]
    edge = tile_cot.shape[4]
    owners, capacity = tile_cot.shape[2], tile_cot.shape[3]
    assert depth == edge and rows == edge and rows % 2 == 0
    lanes = 2 * channels
    pairs = width // lanes
    period = edge // 2
    slots = owners * capacity
    n_gz, n_xy = lax.axis_size("gz"), lax.axis_size("xy")
    n_x = max(n_gz // 2, 1)
    if n_xy % n_x:
        n_x = 1
    members, levels = n_gz * n_x, n_xy // n_x
    n_core = 2 if n_gz % 2 == 0 else 1
    paired = [n_core == 2 and wanted for wanted in (False, False, True, True)]
    joined = [n_core == 2 and wanted for wanted in (True, True, False, False)]

    vol = volume.reshape(depth, rows, pairs, lanes).transpose(0, 2, 1, 3)
    cot = tile_cot.reshape(slots, edge, edge, period, lanes).transpose(0, 1, 3, 2, 4)
    slot = tile_slot.reshape(owners, capacity).T
    count = tile_count.reshape(owners, owners)

    chunks, counts = [], []
    for number, tiles in enumerate((8, 7, 8, 6)):
        counts.append(members // 2 if paired[number] else members)
        chunks.append(-(-tiles * channels // (members * 16)) * 16)
    framed = pltpu.VMEM((depth + 2, rows + 2, pairs, 2 * lanes), BF16)
    band = pltpu.VMEM((48 * channels, 2 * lanes), BF16)
    wide = jax.ShapeDtypeStruct((channels, 27 * channels), F32)
    small = jax.ShapeDtypeStruct((channels, channels), F32)
    cells = depth * rows * pairs
    dma = pltpu.SemaphoreType.DMA
    step = 4 if depth % 4 == 0 else depth
    operands = (vol, cot, backbone_weight, refine_weight, mix_weight, slot, count)
    sums = [pltpu.VMEM((members * chunk, lanes), BF16) for chunk in chunks]
    pieces = []
    for number, (chunk, peers) in enumerate(zip(chunks, counts)):
        pieces += [
            sums[number],
            pltpu.VMEM((peers * chunk, lanes), BF16),
            pltpu.VMEM((peers * chunk, lanes), BF16),
            pltpu.VMEM((peers - 1, chunk, lanes), BF16),
            pltpu.VMEM((levels, chunk, lanes), BF16),
            dma((5,)),
            dma((5,)),
        ]
    vgrad, tot_2, tot_3, refine_step, mix_step = pl.pallas_call(
        functools.partial(step_kernel, n_gz, n_xy, n_x, n_core, paired, joined, period),
        out_shape=(
            jax.ShapeDtypeStruct(vol.shape, BF16),
            jax.ShapeDtypeStruct((members * chunks[2], lanes), BF16),
            jax.ShapeDtypeStruct((members * chunks[3], lanes), BF16),
            wide,
            small,
        ),
        in_specs=[HBM] * 7,
        out_specs=(VMEM,) * 5,
        scratch_shapes=[
            pltpu.VMEM(vol.shape, BF16),
            pltpu.VMEM(cot.shape, BF16),
            pltpu.VMEM(backbone_weight.shape, BF16),
            pltpu.VMEM(refine_weight.shape, BF16),
            pltpu.VMEM(mix_weight.shape, BF16),
            pltpu.SMEM(slot.shape, jnp.int32),
            pltpu.SMEM(count.shape, jnp.int32),
            pltpu.VMEM((cells, lanes), F32),
            pltpu.VMEM((depth // step, rows // 2, step, pairs, 2 * lanes), F32),
            framed, framed, framed, framed,
            band, band, band, band,
            pltpu.VMEM((cells // 2, 2 * lanes), BF16),
            pltpu.VMEM((cells // 2, 2 * lanes), BF16),
            sums[0],
            sums[1],
            dma((7,)),
            dma((8,)), dma((8,)), dma((8,)),
        ]
        + pieces,
        compiler_params=pltpu.CompilerParams(
            collective_id=0, has_side_effects=True, vmem_limit_bytes=32 * 1024 * 1024
        ),
    )(*[pltpu.with_memory_space_constraint(operand, pltpu.HBM) for operand in operands])
    vgrad, back_step, refine_step, mix_step = pl.pallas_call(
        finish_kernel,
        out_shape=(jax.ShapeDtypeStruct(vol.shape, BF16), wide, wide, small),
        in_specs=[VMEM] * 5,
        out_specs=(ANY,) * 4,
        scratch_shapes=[pltpu.VMEM(wide.shape, F32), dma((4,))],
        compiler_params=pltpu.CompilerParams(vmem_limit_bytes=8 * 1024 * 1024),
    )(vgrad, refine_step, mix_step, tot_2, tot_3)
    vgrad = vgrad.transpose(0, 2, 1, 3).reshape(depth, rows, width)
    return (vgrad, back_step, refine_step, mix_step)


def solution(mesh):
    in_specs = (
        P("gz", "xy", None),
        P(),
        P(),
        P(),
        P("gz", "xy", None, None, None, None, None),
        P("gz", "xy", None, None),
        P("gz", None, None),
    )
    out_specs = (P("gz", "xy", None), P(), P(), P())
    return jax.shard_map(body, mesh=mesh, in_specs=in_specs, out_specs=out_specs, check_vma=False)
```

```python
import functools

import jax
import jax.numpy as jnp
from jax import lax
from jax.experimental import pallas as pl
from jax.experimental.pallas import tpu as pltpu
from jax.sharding import PartitionSpec as P

EPSILON = 1e-06
F32 = jnp.float32
BF16 = jnp.bfloat16
VMEM = pl.BlockSpec(memory_space=pltpu.VMEM)
ANY = pl.BlockSpec(memory_space=pl.ANY)
HBM = pl.BlockSpec(memory_space=pltpu.HBM)
MESH = pl.DeviceIdType.MESH


def neighbours():
    return [(dz, dy) for dz in (-1, 0, 1) for dy in (-1, 0, 1) if (dz, dy) != (0, 0)]


def near(step, size):
    if step == 0:
        return pl.ds(1, size)
    return pl.ds(size, 1) if step > 0 else pl.ds(1, 1)


def far(step, size):
    if step == 0:
        return pl.ds(1, size)
    return pl.ds(0, 1) if step > 0 else pl.ds(size + 1, 1)


class Rims:
    def __init__(self, sizes, place, framed, depth, rows, lanes, send, recv):
        self.sizes, self.place, self.framed = sizes, place, framed
        self.depth, self.rows, self.lanes = depth, rows, lanes
        self.send, self.recv = send, recv

    def there(self, dz, dy):
        (n_gz, n_xy), (gz, xy) = self.sizes, self.place
        inside = (gz + dz >= 0) & (gz + dz < n_gz) & (xy + dy >= 0) & (xy + dy < n_xy)
        return inside, (gz + dz, xy + dy)

    def copy(self, dz, dy, number):
        cells = (slice(None), pl.ds(0, self.lanes))
        return pltpu.make_async_remote_copy(
            src_ref=self.framed.at[(near(dz, self.depth), near(dy, self.rows)) + cells],
            dst_ref=self.framed.at[(far(dz, self.depth), far(dy, self.rows)) + cells],
            send_sem=self.send.at[number],
            recv_sem=self.recv.at[number],
            device_id=self.there(dz, dy)[1],
            device_id_type=MESH,
        )

    def start(self):
        for number, (dz, dy) in enumerate(neighbours()):

            @pl.when(self.there(dz, dy)[0])
            def _():
                self.copy(dz, dy, number).start()

    def wait_recv(self):
        for number, (dz, dy) in enumerate(neighbours()):

            @pl.when(self.there(-dz, -dy)[0])
            def _():
                self.copy(dz, dy, number).wait_recv()

    def wait_send(self):
        for number, (dz, dy) in enumerate(neighbours()):

            @pl.when(self.there(dz, dy)[0])
            def _():
                self.copy(dz, dy, number).wait_send()


class Plane:
    def __init__(self, n_gz, n_xy, n_x, n_core):
        gz, xy = lax.axis_index("gz"), lax.axis_index("xy")
        self.gz, self.xy, self.n_x, self.n_core = gz, xy, n_x, n_core
        self.members, self.levels = n_gz * n_x, n_xy // n_x
        self.chips = self.members // n_core
        self.level, self.x = lax.div(xy, n_x), lax.rem(xy, n_x)
        self.core = lax.rem(gz, n_core)
        self.chip = lax.div(gz, n_core) * n_x + self.x
        self.me = self.core * self.chips + self.chip

    def member(self, step):
        who = lax.rem(self.me + step, self.members)
        core, chip = lax.div(who, self.chips), lax.rem(who, self.chips)
        gz = lax.div(chip, self.n_x) * self.n_core + core
        return who, (gz, self.level * self.n_x + lax.rem(chip, self.n_x))

    def other_chip(self, step):
        who = lax.rem(self.chip + step, self.chips)
        gz = lax.div(who, self.n_x) * self.n_core + self.core
        return who, (gz, self.level * self.n_x + lax.rem(who, self.n_x))

    def other_core(self):
        return self.gz + 1 - 2 * self.core, self.xy

    def above(self, step):
        level = lax.rem(self.level + step, self.levels)
        return self.gz, level * self.n_x + self.x


def stages_of(paired, joined):
    return [0] * paired + [1, 2, 3] + [4] * joined


class Total:
    def __init__(self, plane, paired, joined, out, sums, mate, half_sum, got, level_got, send, recv):
        self.joined = joined
        self.stages = stages_of(paired, joined)
        self.plane, self.paired, self.sums, self.mate, self.half_sum = plane, paired, sums, mate, half_sum
        self.got, self.level_got, self.out, self.send, self.recv = got, level_got, out, send, recv
        self.chunk = got.shape[1]
        self.count = plane.chips if paired else plane.members
        self.span = self.count * self.chunk
        base = plane.core * plane.chips * self.chunk
        self.half = pl.ds(pl.multiple_of(base, self.chunk), plane.chips * self.chunk)
        here = plane.chip if paired else plane.me
        self.mine = pl.ds(pl.multiple_of(here * self.chunk, self.chunk), self.chunk)
        self.own = pl.ds(pl.multiple_of(plane.me * self.chunk, self.chunk), self.chunk)
        self.readers = plane.chips if joined else plane.members

    def peer(self, step):
        return self.plane.other_chip(step) if self.paired else self.plane.member(step)

    def remote(self, stage, source, target, device):
        return pltpu.make_async_remote_copy(
            src_ref=source,
            dst_ref=target,
            send_sem=self.send.at[self.stages.index(stage)],
            recv_sem=self.recv.at[self.stages.index(stage)],
            device_id=device,
            device_id_type=MESH,
        )

    def whole(self, stage):
        if stage == 0:
            ref, device = self.mate, self.plane.other_core()
        elif stage == 4:
            ref, device = self.out.at[self.half], self.plane.other_core()
        elif stage == 3:
            ref = self.out.at[pl.ds(0, (self.readers - 1) * self.chunk)]
            device = self.plane.member(1)[1]
        elif stage == 2:
            ref, device = self.level_got.at[pl.ds(0, self.plane.levels - 1)], self.plane.above(1)
        else:
            ref, device = self.got, self.peer(1)[1]
        return self.remote(stage, ref, ref, device)

    def start(self):
        if self.paired:
            other = (1 - self.plane.core) * self.span
            other = pl.ds(pl.multiple_of(other, self.chunk), self.span)
            self.remote(0, self.sums.at[other], self.mate, self.plane.other_core()).start()
        else:
            self.scatter(self.sums)

    def scatter(self, source):
        for step in range(1, self.count):
            who, device = self.peer(step)
            part = pl.ds(pl.multiple_of(who * self.chunk, self.chunk), self.chunk)
            self.remote(1, source.at[part], self.got.at[step - 1], device).start()

    def pair(self):
        if self.paired:
            self.whole(0).wait_recv()
            total = self.sums[self.half, :].astype(F32) + self.mate[...].astype(F32)
            self.half_sum[...] = total.astype(BF16)
            self.scatter(self.half_sum)

    def middle(self):
        self.whole(1).wait_recv()
        total = (self.half_sum if self.paired else self.sums)[self.mine, :].astype(F32)
        for step in range(1, self.count):
            total = total + self.got[step - 1].astype(F32)
        here = self.level_got.at[self.plane.level]
        self.level_got[self.plane.level] = total.astype(BF16)
        for step in range(1, self.plane.levels):
            self.remote(2, here, here, self.plane.above(step)).start()

    def spread(self):
        self.whole(2).wait_recv()
        total = self.level_got[0].astype(F32)
        for level in range(1, self.plane.levels):
            total = total + self.level_got[level].astype(F32)
        self.out[self.own, :] = total.astype(BF16)
        here = self.out.at[self.own]
        for step in range(1, self.readers):
            reader = self.plane.other_chip(step) if self.joined else self.plane.member(step)
            self.remote(3, here, here, reader[1]).start()

    def finish(self):
        self.whole(3).wait_recv()
        if self.joined:
            here = self.out.at[self.half]
            self.remote(4, here, here, self.plane.other_core()).start()

    def end(self):
        if self.joined:
            self.whole(4).wait_recv()

    def drain(self):
        for stage in self.stages:
            self.whole(stage).wait_send()


def weight_halves(weight, half, turned):
    lows, highs = [], []
    count = weight.shape[1] // half
    for first in range(0, count, 2):
        if first + 1 < count:
            near = weight[:, pl.ds(first * half, 2 * half)].astype(F32)
        else:
            last = weight[:, pl.ds(first * half, half)].astype(F32)
            near = jnp.concatenate([last, jnp.zeros_like(last)], axis=1)
        far = pltpu.roll(near, half, 1)
        if turned:
            both = jnp.concatenate([near, far], axis=0).T
            near, far = both[:half], both[half:]
        lows += [near, far]
        highs += [far, near]
    return lows, highs


def fill_band(target, weight, turned):
    half = weight.shape[0]
    lanes = 2 * half
    lows, highs = weight_halves(weight, half, turned)
    low = lax.broadcasted_iota(jnp.int32, (half, lanes), 1) < half
    for offset in range(9):
        ks = [26 - 3 * offset - x if turned else 3 * offset + x for x in range(3)]
        parts = [
            jnp.where(low, lows[ks[1]], highs[ks[0]]),
            jnp.where(low, lows[ks[2]], highs[ks[1]]),
            jnp.where(low, 0.0, highs[ks[2]]),
            jnp.where(low, lows[ks[0]], 0.0),
        ]
        tile = 4 * (offset // 3) + offset % 3
        for place, part in enumerate(parts):
            part = part.astype(BF16)
            target[pl.ds((4 * tile + place) * half, half), pl.ds(0, lanes)] = part
            target[pl.ds((4 * tile + 4 + place) * half, half), pl.ds(lanes, lanes)] = part
    empty = jnp.zeros((4 * half, lanes), BF16)
    for dz in range(3):
        target[pl.ds((4 * dz + 3) * 4 * half, 4 * half), pl.ds(0, lanes)] = empty
        target[pl.ds(4 * dz * 4 * half, 4 * half), pl.ds(lanes, lanes)] = empty


def side_lanes(cells, half, period):
    pairs = cells.shape[1]
    lane = lax.broadcasted_iota(jnp.int32, cells.shape, 2)
    place = lax.broadcasted_iota(jnp.int32, cells.shape, 1) % period
    right = pltpu.roll(cells, pairs - 1, 1)
    left = pltpu.roll(cells, 1, 1)
    low = lane < half
    right = jnp.where(place == period - 1, 0.0, right)
    left = jnp.where(place == 0, 0.0, left)
    return jnp.where(low, right, left)


def window_rows(windows, z, count, dz, dy):
    pairs, width = windows.shape[2], windows.shape[3]
    parts = [
        windows[pl.ds(z + dz, count), y + dy].reshape(count * pairs, width)
        for y in range(0, windows.shape[1] - 2, 2)
    ]
    return jnp.concatenate(parts, axis=0)


def conv_rows(windows, weight, z, count):
    parts = [window_rows(windows, z, count, dz, dy) for dz in range(3) for dy in range(4)]
    return jnp.dot(jnp.concatenate(parts, axis=1), weight[...], preferred_element_type=F32)


def outer_sums(parts, split, hook, windows, grads, half):
    depth, rows, pairs, width = windows.shape
    inner = (pl.ds(1, depth - 2), pl.ds(1, rows - 2))
    cells = (depth - 2) * (rows - 2) * pairs
    grad_turned = grads[inner + (slice(None), pl.ds(0, 2 * half))].reshape(cells, 2 * half).T
    lanes = 2 * half
    low = lax.broadcasted_iota(jnp.int32, (half, lanes), 1) < half
    held = {}

    def put(tile, values):
        part, first = (parts[0], 0) if tile < split else (parts[1], split)
        part[pl.ds((tile - first) * half, half), :] = values.astype(BF16)

    def turn(values):
        return pltpu.roll(values, half, 1)

    for dz in range(3):
        for dy in range(3):
            seen = windows[pl.ds(dz, depth - 2), pl.ds(dy, rows - 2)].reshape(cells, width)
            both = jnp.dot(grad_turned, seen, preferred_element_type=F32)
            top_near, top_far = both[:half, :lanes], both[:half, lanes:]
            last_near, last_far = both[half:, :lanes], both[half:, lanes:]
            sums = ((top_far, last_near), (last_near, top_near), (top_near, last_far))
            for dx, (right, left) in enumerate(sums):
                k = 3 * (3 * dz + dy) + dx
                tile = 2 * (k // 4) + k % 2
                if k % 4 < 2:
                    held[tile] = turn(right) + left
                else:
                    pair = jnp.where(low, held.pop(tile), right + turn(left))
                    put(tile, pair)
                    if tile == split - 1:
                        hook()
    for tile, values in held.items():
        put(tile, jnp.where(low, values, 0.0))


def clear_frame(framed):
    depth, rows = framed.shape[0], framed.shape[1]
    for z in (0, depth - 1):
        framed[z] = jnp.zeros(framed.shape[1:], framed.dtype)
    side = (depth - 2, 1) + framed.shape[2:]
    for y in (0, rows - 1):
        framed[pl.ds(1, depth - 2), pl.ds(y, 1)] = jnp.zeros(side, framed.dtype)


def frame_sides(framed, half):
    depth, rows = framed.shape[0], framed.shape[1]
    pairs, lanes = framed.shape[2], 2 * half

    def fill(zs, ys):
        cells = framed[zs, ys, :, pl.ds(0, lanes)].reshape(-1, pairs, lanes).astype(F32)
        turned = side_lanes(cells, half, pairs).astype(BF16)
        framed[zs, ys, :, pl.ds(lanes, lanes)] = turned.reshape(zs.size, ys.size, pairs, lanes)

    for z in (0, depth - 1):
        fill(pl.ds(z, 1), pl.ds(0, rows))
    for y in (0, rows - 1):
        fill(pl.ds(1, depth - 2), pl.ds(y, 1))


def step_kernel(
    n_gz, n_xy, n_x, n_core, paired, joined, period,
    vol_h, cot_h, back_h, refine_h, mix_h, slot_h, count_h,
    vgrad, tot_2, tot_3, refine_step, mix_step,
    vin, cin, back, refine, mix, slot, count,
    tall, cot, xw, fw, pw, gw, wb, wr, wrt, wbt, gate_s, own_s,
    tot_0, tot_1,
    local, rim_send, rim_recv, grad_recv, *pieces,
):
    depth, pairs, rows, lanes = vin.shape
    half = lanes // 2
    slots, tiles = cin.shape[0], pairs // period
    capacity = slot.shape[0]
    step = 4 if depth % 4 == 0 else depth
    couples = rows // 2
    flat = step * couples * pairs
    split = 8
    gz, xy = lax.axis_index("gz"), lax.axis_index("xy")
    place, sizes = (gz, xy), (n_gz, n_xy)
    plane = Plane(n_gz, n_xy, n_x, n_core)
    rims = Rims(sizes, place, xw, depth, rows, lanes, rim_send, rim_recv)
    grad_rims = Rims(sizes, place, gw, depth, rows, lanes, rim_send, grad_recv)
    totals = []
    for number, tot in enumerate((tot_0, tot_1, tot_2, tot_3)):
        totals.append(Total(plane, paired[number], joined[number], tot, *pieces[7 * number : 7 * number + 7]))

    loads = [
        pltpu.make_async_copy(source, target, local.at[number])
        for number, (source, target) in enumerate(
            (
                (vol_h, vin), (back_h, back), (refine_h, refine), (mix_h, mix),
                (slot_h, slot), (count_h, count), (cot_h, cin),
            )
        )
    ]
    for load in loads:
        load.start()
    for framed in (xw, gw, fw, pw):
        clear_frame(framed)

    barrier = pltpu.get_barrier_semaphore()

    def greet(device):
        pl.semaphore_signal(barrier, inc=1, device_id=device, device_id_type=MESH)

    for dz, dy in neighbours():
        inside, where = rims.there(dz, dy)

        @pl.when(inside)
        def _():
            greet(where)

    for hop in range(1, plane.members):
        greet(plane.member(hop)[1])
    for hop in range(1, plane.levels):
        greet(plane.above(hop))

    loads[0].wait()

    def turn_in(z, carry):
        tall[pl.ds(pl.multiple_of(z * pairs * rows, 8), pairs * rows), :] = (
            vin[z].astype(F32).reshape(pairs * rows, lanes)
        )
        for y in range(rows):
            cells = tall[pl.ds(z * pairs * rows + y, pairs, stride=rows), :]
            xw[z + 1, y + 1, :, pl.ds(0, lanes)] = cells.astype(BF16)
        return carry

    lax.fori_loop(0, depth, turn_in, 0)

    across = 1 + lax.min(gz, 1) + lax.min(n_gz - 1 - gz, 1)
    along = 1 + lax.min(xy, 1) + lax.min(n_xy - 1 - xy, 1)
    pl.semaphore_wait(barrier, across * along - 1 + plane.members - 1 + plane.levels - 1)
    rims.start()

    inner = pl.ds(1, rows)

    def own_sides(z, carry):
        cells = xw[z + 1, inner, :, pl.ds(0, lanes)].astype(F32)
        xw[z + 1, inner, :, pl.ds(lanes, lanes)] = side_lanes(cells, half, pairs).astype(BF16)
        return carry

    lax.fori_loop(0, depth, own_sides, 0)
    loads[1].wait()
    fill_band(wb, back, False)
    loads[2].wait()
    fill_band(wr, refine, False)
    fill_band(wrt, refine, True)
    loads[3].wait()
    mixed = mix[...].astype(F32)
    mixed = jnp.concatenate([mixed, jnp.zeros_like(mixed)], axis=1)
    mix2 = jnp.concatenate([mixed, pltpu.roll(mixed, half, 1)], axis=0).T
    blank = jnp.zeros_like(mix2)
    mix4 = jnp.concatenate(
        [jnp.concatenate([mix2, blank], axis=1), jnp.concatenate([blank, mix2], axis=1)], axis=0
    ).astype(BF16)

    for load in loads[4:]:
        load.wait()
    picks = []
    for number in range(slots):
        owner, place_in = number // capacity, number % capacity
        live = place_in < count[xy, owner]
        which = slot[place_in, owner]
        picks.append([jnp.where(live & (which == tile), 1.0, 0.0) for tile in range(tiles)])

    def pick(z, carry):
        held = [None] * tiles
        for number in range(slots):
            cells = cin[number, z].astype(F32)
            for tile in range(tiles):
                term = cells * picks[number][tile]
                held[tile] = term if held[tile] is None else held[tile] + term
        span = period * rows
        for tile in range(tiles):
            start = pl.multiple_of(z * pairs * rows + tile * span, 8)
            tall[pl.ds(start, span), :] = held[tile].reshape(span, lanes)
        for y in range(rows):
            cot[lax.div(z, step), y // 2, lax.rem(z, step), :, pl.ds(y % 2 * lanes, lanes)] = tall[
                pl.ds(z * pairs * rows + y, pairs, stride=rows), :
            ]
        return carry

    lax.fori_loop(0, depth, pick, 0)

    rims.wait_recv()
    frame_sides(xw, half)

    def put(target, z, cells, period):
        for y in range(rows):
            odd, first = y % 2, y // 2 * step * pairs
            own = cells[first : first + step * pairs, odd * lanes : (odd + 1) * lanes]
            own = own.reshape(step, pairs, lanes)
            target[pl.ds(z + 1, step), y + 1, :, pl.ds(0, lanes)] = own
            target[pl.ds(z + 1, step), y + 1, :, pl.ds(lanes, lanes)] = side_lanes(
                own.astype(F32), half, period
            ).astype(BF16)

    def take(framed, z):
        parts = [framed[pl.ds(z + 1, step), y + 1, :, pl.ds(0, lanes)] for y in range(rows)]
        parts = [part.reshape(step * pairs, lanes) for part in parts]
        lines = [jnp.concatenate(parts[odd::2], axis=0) for odd in range(2)]
        return jnp.concatenate(lines, axis=1).astype(F32)

    def line(z):
        return pl.ds(z * couples * pairs, flat)

    for z in range(0, depth, step):
        put(fw, z, (take(xw, z) + conv_rows(xw, wb, z, step)).astype(BF16), period)
    for z in range(0, depth, step):
        pre = conv_rows(fw, wr, z, step)
        sig = jax.nn.sigmoid(pre)
        upstream = cot[z // step].reshape(flat, 2 * lanes).astype(BF16)
        gate_s[line(z), :] = (pre * sig).astype(BF16)
        gated_grad = jnp.dot(upstream, mix4, preferred_element_type=F32)
        pre_grad = (gated_grad * sig * (1.0 + pre * (1.0 - sig))).astype(BF16)
        put(pw, z, pre_grad, period)

    def begin(number):
        part = totals[number].sums
        used = (split if number % 2 == 0 else 15 - split if number == 1 else 14 - split) * half
        if used < part.shape[0]:
            part[pl.ds(used, part.shape[0] - used), :] = jnp.zeros((part.shape[0] - used, lanes), BF16)
        totals[number].start()

    outer_sums((totals[0].sums, totals[1].sums), split, lambda: begin(0), fw, pw, half)
    cot_rows = cot[...].reshape(depth * couples * pairs, 2 * lanes).astype(BF16)
    both = jnp.dot(gate_s[...].T, cot_rows, preferred_element_type=F32)
    both = both[:lanes, :lanes] + both[lanes:, lanes:]
    lane = lax.broadcasted_iota(jnp.int32, (half, lanes), 1)
    totals[1].sums[pl.ds((14 - split) * half, half), :] = jnp.where(
        lane < half, both[:half] + pltpu.roll(both[half:], half, 1), 0.0
    ).astype(BF16)
    begin(1)

    for z in range(0, depth, step):
        upstream = cot[z // step].reshape(flat, 2 * lanes)
        grad = (upstream + conv_rows(pw, wrt, z, step)).astype(BF16)
        own_s[line(z), :] = grad
        put(gw, z, grad, pairs)
    for total in totals[:2]:
        total.pair()

    outer_sums((totals[2].sums, totals[3].sums), split, lambda: begin(2), xw, gw, half)
    begin(3)
    rims.wait_send()

    def back_conv(z):
        grad = own_s[line(z), :].astype(F32) + conv_rows(gw, wbt, z, step)
        grad = grad.reshape(couples, step, pairs, 2 * lanes)
        for y in range(rows):
            for level in range(step):
                tall[pl.ds(((z + level) * rows + y) * pairs, pairs), :] = grad[
                    y // 2, level, :, y % 2 * lanes : (y % 2 + 1) * lanes
                ]

    def turn_out(z, carry):
        for pair in range(pairs):
            cells = tall[pl.ds(z * pairs * rows + pair, rows, stride=pairs), :]
            vgrad[z, pair] = cells.astype(BF16)
        return carry

    grad_rims.start()
    fill_band(wbt, back, True)
    for total in totals[2:]:
        total.pair()
    for total in totals[:2]:
        total.middle()
    for total in totals[2:]:
        total.middle()
    for total in totals[:2]:
        total.spread()
    grad_rims.wait_recv()
    frame_sides(gw, half)
    back_conv(0)
    for z in range(step, depth, step):
        back_conv(z)
    lax.fori_loop(0, depth, turn_out, 0)
    for total in totals[2:]:
        total.spread()
    for total in totals[:2]:
        total.finish()
    for total in totals[:2]:
        total.end()
    write_step(tot_0, tot_1, split, refine_step, half)
    values = tot_1[pl.ds((14 - split) * half, half), :].astype(F32)
    mix_step[...] = (values / scale_of(values, 1.0 * half * half))[:, :half]
    for total in totals[2:]:
        total.finish()
    for total in totals[2:]:
        total.end()
    grad_rims.wait_send()
    for total in totals:
        total.drain()


def scale_of(values, count):
    squares = jnp.sum(values * values, axis=0, keepdims=True)
    return jnp.sqrt(jnp.sum(squares, axis=1, keepdims=True) / count + EPSILON)


def write_step(first, second, split, out, half):
    lanes = 2 * half
    values = jnp.concatenate(
        [first[pl.ds(0, split * half), :], second[pl.ds(0, (14 - split) * half), :]], axis=0
    ).astype(F32)
    scale = scale_of(values, 27.0 * half * half)
    for quad in range(7):
        turned = values[quad * lanes : (quad + 1) * lanes].T / scale
        out[:, pl.ds(quad * 2 * lanes, lanes)] = turned[:half]
        wide = min(lanes, out.shape[1] - quad * 2 * lanes - lanes)
        out[:, pl.ds(quad * 2 * lanes + lanes, wide)] = turned[half:, :wide]


def finish_kernel(
    vgrad, refine_step, mix_step, tot_2, tot_3, vgrad_out, back_out, refine_out, mix_out, back_step, sems
):
    copies = [
        pltpu.make_async_copy(source, target, sems.at[number])
        for number, (source, target) in enumerate(
            ((vgrad, vgrad_out), (refine_step, refine_out), (mix_step, mix_out), (back_step, back_out))
        )
    ]
    for copy in copies[:3]:
        copy.start()
    write_step(tot_2, tot_3, 8, back_step, mix_step.shape[0])
    copies[3].start()
    for copy in copies:
        copy.wait()


def body(volume, backbone_weight, refine_weight, mix_weight, tile_cot, tile_slot, tile_count):
    depth, rows, width = volume.shape
    channels = mix_weight.shape[0]
    edge = tile_cot.shape[4]
    owners, capacity = tile_cot.shape[2], tile_cot.shape[3]
    assert depth == edge and rows == edge and rows % 2 == 0
    lanes = 2 * channels
    pairs = width // lanes
    period = edge // 2
    slots = owners * capacity
    n_gz, n_xy = lax.axis_size("gz"), lax.axis_size("xy")
    n_x = max(n_gz // 2, 1)
    if n_xy % n_x:
        n_x = 1
    members, levels = n_gz * n_x, n_xy // n_x
    n_core = 2 if n_gz % 2 == 0 else 1
    paired = [n_core == 2 and wanted for wanted in (False, False, True, True)]
    joined = [n_core == 2 and wanted for wanted in (True, True, False, False)]

    vol = volume.reshape(depth, rows, pairs, lanes).transpose(0, 2, 1, 3)
    cot = tile_cot.reshape(slots, edge, edge, period, lanes).transpose(0, 1, 3, 2, 4)
    slot = tile_slot.reshape(owners, capacity).T
    count = tile_count.reshape(owners, owners)

    chunks, counts = [], []
    for number, tiles in enumerate((8, 7, 8, 6)):
        counts.append(members // 2 if paired[number] else members)
        chunks.append(-(-tiles * channels // (members * 16)) * 16)
    framed = pltpu.VMEM((depth + 2, rows + 2, pairs, 2 * lanes), BF16)
    band = pltpu.VMEM((48 * channels, 2 * lanes), BF16)
    wide = jax.ShapeDtypeStruct((channels, 27 * channels), F32)
    small = jax.ShapeDtypeStruct((channels, channels), F32)
    cells = depth * rows * pairs
    dma = pltpu.SemaphoreType.DMA
    step = 4 if depth % 4 == 0 else depth
    operands = (vol, cot, backbone_weight, refine_weight, mix_weight, slot, count)
    sums = [pltpu.VMEM((members * chunk, lanes), BF16) for chunk in chunks]
    pieces = []
    for number, (chunk, peers) in enumerate(zip(chunks, counts)):
        pieces += [
            sums[number],
            pltpu.VMEM((peers * chunk, lanes), BF16),
            pltpu.VMEM((peers * chunk, lanes), BF16),
            pltpu.VMEM((peers - 1, chunk, lanes), BF16),
            pltpu.VMEM((levels, chunk, lanes), BF16),
            dma((len(stages_of(paired[number], joined[number])),)),
            dma((len(stages_of(paired[number], joined[number])),)),
        ]
    vgrad, tot_2, tot_3, refine_step, mix_step = pl.pallas_call(
        functools.partial(step_kernel, n_gz, n_xy, n_x, n_core, paired, joined, period),
        out_shape=(
            jax.ShapeDtypeStruct(vol.shape, BF16),
            jax.ShapeDtypeStruct((members * chunks[2], lanes), BF16),
            jax.ShapeDtypeStruct((members * chunks[3], lanes), BF16),
            wide,
            small,
        ),
        in_specs=[HBM] * 7,
        out_specs=(VMEM,) * 5,
        scratch_shapes=[
            pltpu.VMEM(vol.shape, BF16),
            pltpu.VMEM(cot.shape, BF16),
            pltpu.VMEM(backbone_weight.shape, BF16),
            pltpu.VMEM(refine_weight.shape, BF16),
            pltpu.VMEM(mix_weight.shape, BF16),
            pltpu.SMEM(slot.shape, jnp.int32),
            pltpu.SMEM(count.shape, jnp.int32),
            pltpu.VMEM((cells, lanes), F32),
            pltpu.VMEM((depth // step, rows // 2, step, pairs, 2 * lanes), F32),
            framed, framed, framed, framed,
            band, band, band, band,
            pltpu.VMEM((cells // 2, 2 * lanes), BF16),
            pltpu.VMEM((cells // 2, 2 * lanes), BF16),
            sums[0],
            sums[1],
            dma((7,)),
            dma((8,)), dma((8,)), dma((8,)),
        ]
        + pieces,
        compiler_params=pltpu.CompilerParams(
            collective_id=0, has_side_effects=True, vmem_limit_bytes=32 * 1024 * 1024
        ),
    )(*[pltpu.with_memory_space_constraint(operand, pltpu.HBM) for operand in operands])
    vgrad, back_step, refine_step, mix_step = pl.pallas_call(
        finish_kernel,
        out_shape=(jax.ShapeDtypeStruct(vol.shape, BF16), wide, wide, small),
        in_specs=[VMEM] * 5,
        out_specs=(ANY,) * 4,
        scratch_shapes=[pltpu.VMEM(wide.shape, F32), dma((4,))],
        compiler_params=pltpu.CompilerParams(vmem_limit_bytes=8 * 1024 * 1024),
    )(vgrad, refine_step, mix_step, tot_2, tot_3)
    vgrad = vgrad.transpose(0, 2, 1, 3).reshape(depth, rows, width)
    return (vgrad, back_step, refine_step, mix_step)


def solution(mesh):
    in_specs = (
        P("gz", "xy", None),
        P(),
        P(),
        P(),
        P("gz", "xy", None, None, None, None, None),
        P("gz", "xy", None, None),
        P("gz", None, None),
    )
    out_specs = (P("gz", "xy", None), P(), P(), P())
    return jax.shard_map(body, mesh=mesh, in_specs=in_specs, out_specs=out_specs, check_vma=False)
```

```python
import functools

import jax
import jax.numpy as jnp
from jax import lax
from jax.experimental import pallas as pl
from jax.experimental.pallas import tpu as pltpu
from jax.sharding import PartitionSpec as P

EPSILON = 1e-06
F32 = jnp.float32
BF16 = jnp.bfloat16
VMEM = pl.BlockSpec(memory_space=pltpu.VMEM)
ANY = pl.BlockSpec(memory_space=pl.ANY)
HBM = pl.BlockSpec(memory_space=pltpu.HBM)
MESH = pl.DeviceIdType.MESH


def neighbours():
    return [(dz, dy) for dz in (-1, 0, 1) for dy in (-1, 0, 1) if (dz, dy) != (0, 0)]


def near(step, size):
    if step == 0:
        return pl.ds(1, size)
    return pl.ds(size, 1) if step > 0 else pl.ds(1, 1)


def far(step, size):
    if step == 0:
        return pl.ds(1, size)
    return pl.ds(0, 1) if step > 0 else pl.ds(size + 1, 1)


class Rims:
    def __init__(self, sizes, place, framed, depth, rows, lanes, send, recv):
        self.sizes, self.place, self.framed = sizes, place, framed
        self.depth, self.rows, self.lanes = depth, rows, lanes
        self.send, self.recv = send, recv

    def there(self, dz, dy):
        (n_gz, n_xy), (gz, xy) = self.sizes, self.place
        inside = (gz + dz >= 0) & (gz + dz < n_gz) & (xy + dy >= 0) & (xy + dy < n_xy)
        return inside, (gz + dz, xy + dy)

    def copy(self, dz, dy, number):
        cells = (slice(None), pl.ds(0, self.lanes))
        return pltpu.make_async_remote_copy(
            src_ref=self.framed.at[(near(dz, self.depth), near(dy, self.rows)) + cells],
            dst_ref=self.framed.at[(far(dz, self.depth), far(dy, self.rows)) + cells],
            send_sem=self.send.at[number],
            recv_sem=self.recv.at[number],
            device_id=self.there(dz, dy)[1],
            device_id_type=MESH,
        )

    def start(self):
        for number, (dz, dy) in enumerate(neighbours()):

            @pl.when(self.there(dz, dy)[0])
            def _():
                self.copy(dz, dy, number).start()

    def wait_recv(self):
        for number, (dz, dy) in enumerate(neighbours()):

            @pl.when(self.there(-dz, -dy)[0])
            def _():
                self.copy(dz, dy, number).wait_recv()

    def wait_send(self):
        for number, (dz, dy) in enumerate(neighbours()):

            @pl.when(self.there(dz, dy)[0])
            def _():
                self.copy(dz, dy, number).wait_send()


class Plane:
    def __init__(self, n_gz, n_xy, n_x, n_core):
        gz, xy = lax.axis_index("gz"), lax.axis_index("xy")
        self.gz, self.xy, self.n_x, self.n_core = gz, xy, n_x, n_core
        self.members, self.levels = n_gz * n_x, n_xy // n_x
        self.chips = self.members // n_core
        self.level, self.x = lax.div(xy, n_x), lax.rem(xy, n_x)
        self.core = lax.rem(gz, n_core)
        self.chip = lax.div(gz, n_core) * n_x + self.x
        self.me = self.core * self.chips + self.chip

    def member(self, step):
        who = lax.rem(self.me + step, self.members)
        core, chip = lax.div(who, self.chips), lax.rem(who, self.chips)
        gz = lax.div(chip, self.n_x) * self.n_core + core
        return who, (gz, self.level * self.n_x + lax.rem(chip, self.n_x))

    def other_chip(self, step):
        who = lax.rem(self.chip + step, self.chips)
        gz = lax.div(who, self.n_x) * self.n_core + self.core
        return who, (gz, self.level * self.n_x + lax.rem(who, self.n_x))

    def other_core(self):
        return self.gz + 1 - 2 * self.core, self.xy

    def above(self, step):
        level = lax.rem(self.level + step, self.levels)
        return self.gz, level * self.n_x + self.x


def stages_of(paired, joined):
    return [0] * paired + [1, 2, 3] + [4] * joined


class Total:
    def __init__(self, plane, paired, joined, out, sums, mate, half_sum, got, level_got, send, recv):
        self.joined = joined
        self.stages = stages_of(paired, joined)
        self.plane, self.paired, self.sums, self.mate, self.half_sum = plane, paired, sums, mate, half_sum
        self.got, self.level_got, self.out, self.send, self.recv = got, level_got, out, send, recv
        self.chunk = got.shape[1]
        self.count = plane.chips if paired else plane.members
        self.span = self.count * self.chunk
        base = plane.core * plane.chips * self.chunk
        self.half = pl.ds(pl.multiple_of(base, self.chunk), plane.chips * self.chunk)
        here = plane.chip if paired else plane.me
        self.mine = pl.ds(pl.multiple_of(here * self.chunk, self.chunk), self.chunk)
        self.own = pl.ds(pl.multiple_of(plane.me * self.chunk, self.chunk), self.chunk)
        self.readers = plane.chips if joined else plane.members

    def peer(self, step):
        return self.plane.other_chip(step) if self.paired else self.plane.member(step)

    def remote(self, stage, source, target, device):
        return pltpu.make_async_remote_copy(
            src_ref=source,
            dst_ref=target,
            send_sem=self.send.at[self.stages.index(stage)],
            recv_sem=self.recv.at[self.stages.index(stage)],
            device_id=device,
            device_id_type=MESH,
        )

    def whole(self, stage):
        if stage == 0:
            ref, device = self.mate, self.plane.other_core()
        elif stage == 4:
            ref, device = self.out.at[self.half], self.plane.other_core()
        elif stage == 3:
            ref = self.out.at[pl.ds(0, (self.readers - 1) * self.chunk)]
            device = self.plane.member(1)[1]
        elif stage == 2:
            ref, device = self.level_got.at[pl.ds(0, self.plane.levels - 1)], self.plane.above(1)
        else:
            ref, device = self.got, self.peer(1)[1]
        return self.remote(stage, ref, ref, device)

    def start(self):
        if self.paired:
            other = (1 - self.plane.core) * self.span
            other = pl.ds(pl.multiple_of(other, self.chunk), self.span)
            self.remote(0, self.sums.at[other], self.mate, self.plane.other_core()).start()
        else:
            self.scatter(self.sums)

    def scatter(self, source):
        for step in range(1, self.count):
            who, device = self.peer(step)
            part = pl.ds(pl.multiple_of(who * self.chunk, self.chunk), self.chunk)
            self.remote(1, source.at[part], self.got.at[step - 1], device).start()

    def pair(self):
        if self.paired:
            self.whole(0).wait_recv()
            total = self.sums[self.half, :].astype(F32) + self.mate[...].astype(F32)
            self.half_sum[...] = total.astype(BF16)
            self.scatter(self.half_sum)

    def middle(self):
        self.whole(1).wait_recv()
        total = (self.half_sum if self.paired else self.sums)[self.mine, :].astype(F32)
        for step in range(1, self.count):
            total = total + self.got[step - 1].astype(F32)
        here = self.level_got.at[self.plane.level]
        self.level_got[self.plane.level] = total.astype(BF16)
        for step in range(1, self.plane.levels):
            self.remote(2, here, here, self.plane.above(step)).start()

    def spread(self):
        self.whole(2).wait_recv()
        total = self.level_got[0].astype(F32)
        for level in range(1, self.plane.levels):
            total = total + self.level_got[level].astype(F32)
        self.out[self.own, :] = total.astype(BF16)
        here = self.out.at[self.own]
        for step in range(1, self.readers):
            reader = self.plane.other_chip(step) if self.joined else self.plane.member(step)
            self.remote(3, here, here, reader[1]).start()

    def finish(self):
        self.whole(3).wait_recv()
        if self.joined:
            here = self.out.at[self.half]
            self.remote(4, here, here, self.plane.other_core()).start()

    def end(self):
        if self.joined:
            self.whole(4).wait_recv()

    def drain(self):
        for stage in self.stages:
            self.whole(stage).wait_send()


def weight_halves(weight, half, turned):
    lows, highs = [], []
    count = weight.shape[1] // half
    for first in range(0, count, 2):
        if first + 1 < count:
            near = weight[:, pl.ds(first * half, 2 * half)].astype(F32)
        else:
            last = weight[:, pl.ds(first * half, half)].astype(F32)
            near = jnp.concatenate([last, jnp.zeros_like(last)], axis=1)
        far = pltpu.roll(near, half, 1)
        if turned:
            both = jnp.concatenate([near, far], axis=0).T
            near, far = both[:half], both[half:]
        lows += [near, far]
        highs += [far, near]
    return lows, highs


def fill_band(target, weight, turned):
    half = weight.shape[0]
    lanes = 2 * half
    lows, highs = weight_halves(weight, half, turned)
    low = lax.broadcasted_iota(jnp.int32, (half, lanes), 1) < half
    for offset in range(9):
        ks = [26 - 3 * offset - x if turned else 3 * offset + x for x in range(3)]
        parts = [
            jnp.where(low, lows[ks[1]], highs[ks[0]]),
            jnp.where(low, lows[ks[2]], highs[ks[1]]),
            jnp.where(low, 0.0, highs[ks[2]]),
            jnp.where(low, lows[ks[0]], 0.0),
        ]
        tile = 4 * (offset // 3) + offset % 3
        for place, part in enumerate(parts):
            part = part.astype(BF16)
            target[pl.ds((4 * tile + place) * half, half), pl.ds(0, lanes)] = part
            target[pl.ds((4 * tile + 4 + place) * half, half), pl.ds(lanes, lanes)] = part
    empty = jnp.zeros((4 * half, lanes), BF16)
    for dz in range(3):
        target[pl.ds((4 * dz + 3) * 4 * half, 4 * half), pl.ds(0, lanes)] = empty
        target[pl.ds(4 * dz * 4 * half, 4 * half), pl.ds(lanes, lanes)] = empty


def side_lanes(cells, half, period):
    pairs = cells.shape[1]
    lane = lax.broadcasted_iota(jnp.int32, cells.shape, 2)
    place = lax.broadcasted_iota(jnp.int32, cells.shape, 1) % period
    right = pltpu.roll(cells, pairs - 1, 1)
    left = pltpu.roll(cells, 1, 1)
    low = lane < half
    right = jnp.where(place == period - 1, 0.0, right)
    left = jnp.where(place == 0, 0.0, left)
    return jnp.where(low, right, left)


def window_rows(windows, z, count, dz, dy):
    pairs, width = windows.shape[2], windows.shape[3]
    parts = [
        windows[pl.ds(z + dz, count), y + dy].reshape(count * pairs, width)
        for y in range(0, windows.shape[1] - 2, 2)
    ]
    return jnp.concatenate(parts, axis=0)


def conv_rows(windows, weight, z, count):
    parts = [window_rows(windows, z, count, dz, dy) for dz in range(3) for dy in range(4)]
    return jnp.dot(jnp.concatenate(parts, axis=1), weight[...], preferred_element_type=F32)


def outer_sums(parts, split, hook, windows, grads, half):
    depth, rows, pairs, width = windows.shape
    inner = (pl.ds(1, depth - 2), pl.ds(1, rows - 2))
    cells = (depth - 2) * (rows - 2) * pairs
    grad_turned = grads[inner + (slice(None), pl.ds(0, 2 * half))].reshape(cells, 2 * half).T
    lanes = 2 * half
    low = lax.broadcasted_iota(jnp.int32, (half, lanes), 1) < half
    held = {}

    def put(tile, values):
        part, first = (parts[0], 0) if tile < split else (parts[1], split)
        part[pl.ds((tile - first) * half, half), :] = values.astype(BF16)

    def turn(values):
        return pltpu.roll(values, half, 1)

    for dz in range(3):
        for dy in range(3):
            seen = windows[pl.ds(dz, depth - 2), pl.ds(dy, rows - 2)].reshape(cells, width)
            both = jnp.dot(grad_turned, seen, preferred_element_type=F32)
            top_near, top_far = both[:half, :lanes], both[:half, lanes:]
            last_near, last_far = both[half:, :lanes], both[half:, lanes:]
            sums = ((top_far, last_near), (last_near, top_near), (top_near, last_far))
            for dx, (right, left) in enumerate(sums):
                k = 3 * (3 * dz + dy) + dx
                tile = 2 * (k // 4) + k % 2
                if k % 4 < 2:
                    held[tile] = turn(right) + left
                else:
                    pair = jnp.where(low, held.pop(tile), right + turn(left))
                    put(tile, pair)
                    if tile == split - 1:
                        hook()
    for tile, values in held.items():
        put(tile, jnp.where(low, values, 0.0))


def clear_frame(framed):
    depth, rows = framed.shape[0], framed.shape[1]
    for z in (0, depth - 1):
        framed[z] = jnp.zeros(framed.shape[1:], framed.dtype)
    side = (depth - 2, 1) + framed.shape[2:]
    for y in (0, rows - 1):
        framed[pl.ds(1, depth - 2), pl.ds(y, 1)] = jnp.zeros(side, framed.dtype)


def frame_sides(framed, half):
    depth, rows = framed.shape[0], framed.shape[1]
    pairs, lanes = framed.shape[2], 2 * half

    def fill(zs, ys):
        cells = framed[zs, ys, :, pl.ds(0, lanes)].reshape(-1, pairs, lanes).astype(F32)
        turned = side_lanes(cells, half, pairs).astype(BF16)
        framed[zs, ys, :, pl.ds(lanes, lanes)] = turned.reshape(zs.size, ys.size, pairs, lanes)

    for z in (0, depth - 1):
        fill(pl.ds(z, 1), pl.ds(0, rows))
    for y in (0, rows - 1):
        fill(pl.ds(1, depth - 2), pl.ds(y, 1))


def step_kernel(
    n_gz, n_xy, n_x, n_core, paired, joined, period,
    vol_h, cot_h, back_h, refine_h, mix_h, slot_h, count_h,
    vgrad, tot_2, tot_3, refine_step, mix_step,
    vin, cin, back, refine, mix, slot, count,
    tall, cot, xw, fw, pw, gw, wb, wr, wrt, wbt, gate_s, own_s,
    tot_0, tot_1,
    local, rim_send, rim_recv, grad_recv, *pieces,
):
    depth, pairs, rows, lanes = vin.shape
    half = lanes // 2
    slots, tiles = cin.shape[0], pairs // period
    capacity = slot.shape[0]
    step = 4 if depth % 4 == 0 else depth
    couples = rows // 2
    flat = step * couples * pairs
    split = 8
    gz, xy = lax.axis_index("gz"), lax.axis_index("xy")
    place, sizes = (gz, xy), (n_gz, n_xy)
    plane = Plane(n_gz, n_xy, n_x, n_core)
    rims = Rims(sizes, place, xw, depth, rows, lanes, rim_send, rim_recv)
    grad_rims = Rims(sizes, place, gw, depth, rows, lanes, rim_send, grad_recv)
    totals = []
    for number, tot in enumerate((tot_0, tot_1, tot_2, tot_3)):
        totals.append(Total(plane, paired[number], joined[number], tot, *pieces[7 * number : 7 * number + 7]))

    loads = [
        pltpu.make_async_copy(source, target, local.at[number])
        for number, (source, target) in enumerate(
            (
                (vol_h, vin), (back_h, back), (refine_h, refine), (mix_h, mix),
                (slot_h, slot), (count_h, count), (cot_h, cin),
            )
        )
    ]
    for load in loads:
        load.start()
    for framed in (xw, gw, fw, pw):
        clear_frame(framed)

    barrier = pltpu.get_barrier_semaphore()

    def greet(device):
        pl.semaphore_signal(barrier, inc=1, device_id=device, device_id_type=MESH)

    for dz, dy in neighbours():
        inside, where = rims.there(dz, dy)

        @pl.when(inside)
        def _():
            greet(where)

    for hop in range(1, plane.members):
        greet(plane.member(hop)[1])
    for hop in range(1, plane.levels):
        greet(plane.above(hop))

    loads[0].wait()

    def turn_in(z, carry):
        tall[pl.ds(pl.multiple_of(z * pairs * rows, 8), pairs * rows), :] = (
            vin[z].astype(F32).reshape(pairs * rows, lanes)
        )
        for y in range(rows):
            cells = tall[pl.ds(z * pairs * rows + y, pairs, stride=rows), :]
            xw[z + 1, y + 1, :, pl.ds(0, lanes)] = cells.astype(BF16)
        return carry

    lax.fori_loop(0, depth, turn_in, 0)

    across = 1 + lax.min(gz, 1) + lax.min(n_gz - 1 - gz, 1)
    along = 1 + lax.min(xy, 1) + lax.min(n_xy - 1 - xy, 1)
    pl.semaphore_wait(barrier, across * along - 1 + plane.members - 1 + plane.levels - 1)
    rims.start()

    inner = pl.ds(1, rows)

    def own_sides(z, carry):
        cells = xw[z + 1, inner, :, pl.ds(0, lanes)].astype(F32)
        xw[z + 1, inner, :, pl.ds(lanes, lanes)] = side_lanes(cells, half, pairs).astype(BF16)
        return carry

    lax.fori_loop(0, depth, own_sides, 0)
    loads[1].wait()
    fill_band(wb, back, False)
    loads[2].wait()
    fill_band(wr, refine, False)
    fill_band(wrt, refine, True)
    loads[3].wait()
    mixed = mix[...].astype(F32)
    mixed = jnp.concatenate([mixed, jnp.zeros_like(mixed)], axis=1)
    mix2 = jnp.concatenate([mixed, pltpu.roll(mixed, half, 1)], axis=0).T
    blank = jnp.zeros_like(mix2)
    mix4 = jnp.concatenate(
        [jnp.concatenate([mix2, blank], axis=1), jnp.concatenate([blank, mix2], axis=1)], axis=0
    ).astype(BF16)

    for load in loads[4:]:
        load.wait()
    picks = []
    for number in range(slots):
        owner, place_in = number // capacity, number % capacity
        live = place_in < count[xy, owner]
        which = slot[place_in, owner]
        picks.append([jnp.where(live & (which == tile), 1.0, 0.0) for tile in range(tiles)])

    def pick(z, carry):
        held = [None] * tiles
        for number in range(slots):
            cells = cin[number, z].astype(F32)
            for tile in range(tiles):
                term = cells * picks[number][tile]
                held[tile] = term if held[tile] is None else held[tile] + term
        span = period * rows
        for tile in range(tiles):
            start = pl.multiple_of(z * pairs * rows + tile * span, 8)
            tall[pl.ds(start, span), :] = held[tile].reshape(span, lanes)
        for y in range(rows):
            cot[lax.div(z, step), y // 2, lax.rem(z, step), :, pl.ds(y % 2 * lanes, lanes)] = tall[
                pl.ds(z * pairs * rows + y, pairs, stride=rows), :
            ]
        return carry

    lax.fori_loop(0, depth, pick, 0)

    rims.wait_recv()
    frame_sides(xw, half)

    def put(target, z, cells, period):
        for y in range(rows):
            odd, first = y % 2, y // 2 * step * pairs
            own = cells[first : first + step * pairs, odd * lanes : (odd + 1) * lanes]
            own = own.reshape(step, pairs, lanes)
            target[pl.ds(z + 1, step), y + 1, :, pl.ds(0, lanes)] = own
            target[pl.ds(z + 1, step), y + 1, :, pl.ds(lanes, lanes)] = side_lanes(
                own.astype(F32), half, period
            ).astype(BF16)

    def take(framed, z):
        parts = [framed[pl.ds(z + 1, step), y + 1, :, pl.ds(0, lanes)] for y in range(rows)]
        parts = [part.reshape(step * pairs, lanes) for part in parts]
        lines = [jnp.concatenate(parts[odd::2], axis=0) for odd in range(2)]
        return jnp.concatenate(lines, axis=1).astype(F32)

    def line(z):
        return pl.ds(z * couples * pairs, flat)

    for z in range(0, depth, step):
        put(fw, z, (take(xw, z) + conv_rows(xw, wb, z, step)).astype(BF16), period)
    for z in range(0, depth, step):
        pre = conv_rows(fw, wr, z, step)
        sig = jax.nn.sigmoid(pre)
        upstream = cot[z // step].reshape(flat, 2 * lanes).astype(BF16)
        gate_s[line(z), :] = (pre * sig).astype(BF16)
        gated_grad = jnp.dot(upstream, mix4, preferred_element_type=F32)
        pre_grad = (gated_grad * sig * (1.0 + pre * (1.0 - sig))).astype(BF16)
        put(pw, z, pre_grad, period)

    def begin(number):
        part = totals[number].sums
        used = (split if number % 2 == 0 else 15 - split if number == 1 else 14 - split) * half
        if used < part.shape[0]:
            part[pl.ds(used, part.shape[0] - used), :] = jnp.zeros((part.shape[0] - used, lanes), BF16)
        totals[number].start()

    outer_sums((totals[0].sums, totals[1].sums), split, lambda: begin(0), fw, pw, half)
    cot_rows = cot[...].reshape(depth * couples * pairs, 2 * lanes).astype(BF16)
    both = jnp.dot(gate_s[...].T, cot_rows, preferred_element_type=F32)
    both = both[:lanes, :lanes] + both[lanes:, lanes:]
    lane = lax.broadcasted_iota(jnp.int32, (half, lanes), 1)
    totals[1].sums[pl.ds((14 - split) * half, half), :] = jnp.where(
        lane < half, both[:half] + pltpu.roll(both[half:], half, 1), 0.0
    ).astype(BF16)
    begin(1)

    for z in range(0, depth, step):
        upstream = cot[z // step].reshape(flat, 2 * lanes)
        grad = (upstream + conv_rows(pw, wrt, z, step)).astype(BF16)
        own_s[line(z), :] = grad
        put(gw, z, grad, pairs)
    for total in totals[:2]:
        total.pair()

    outer_sums((totals[2].sums, totals[3].sums), split, lambda: begin(2), xw, gw, half)
    begin(3)
    rims.wait_send()

    def back_conv(z):
        grad = own_s[line(z), :].astype(F32) + conv_rows(gw, wbt, z, step)
        grad = grad.reshape(couples, step, pairs, 2 * lanes)
        for y in range(rows):
            for level in range(step):
                tall[pl.ds(((z + level) * rows + y) * pairs, pairs), :] = grad[
                    y // 2, level, :, y % 2 * lanes : (y % 2 + 1) * lanes
                ]

    def turn_out(z, carry):
        for pair in range(pairs):
            cells = tall[pl.ds(z * pairs * rows + pair, rows, stride=pairs), :]
            vgrad[z, pair] = cells.astype(BF16)
        return carry

    grad_rims.start()
    fill_band(wbt, back, True)
    for total in totals[2:]:
        total.pair()
    for total in totals[:2]:
        total.middle()
    for total in totals[2:]:
        total.middle()
    for total in totals[:2]:
        total.spread()
    grad_rims.wait_recv()
    frame_sides(gw, half)
    back_conv(0)
    for z in range(step, depth, step):
        back_conv(z)
    lax.fori_loop(0, depth, turn_out, 0)
    for total in totals[2:]:
        total.spread()
    for total in totals[:2]:
        total.finish()
    for total in totals[:2]:
        total.end()
    write_step(tot_0, tot_1, split, refine_step, half)
    values = tot_1[pl.ds((14 - split) * half, half), :].astype(F32)
    mix_step[...] = (values / scale_of(values, 1.0 * half * half))[:, :half]
    for total in totals[2:]:
        total.finish()
    for total in totals[2:]:
        total.end()
    grad_rims.wait_send()
    for total in totals:
        total.drain()


def scale_of(values, count):
    squares = jnp.sum(values * values, axis=0, keepdims=True)
    return jnp.sqrt(jnp.sum(squares, axis=1, keepdims=True) / count + EPSILON)


def write_step(first, second, split, out, half):
    lanes = 2 * half
    values = jnp.concatenate(
        [first[pl.ds(0, split * half), :], second[pl.ds(0, (14 - split) * half), :]], axis=0
    ).astype(F32)
    scale = 1.0 / scale_of(values, 27.0 * half * half)
    for quad in range(7):
        turned = values[quad * lanes : (quad + 1) * lanes].T * scale
        out[:, pl.ds(quad * 2 * lanes, lanes)] = turned[:half]
        wide = min(lanes, out.shape[1] - quad * 2 * lanes - lanes)
        out[:, pl.ds(quad * 2 * lanes + lanes, wide)] = turned[half:, :wide]


def finish_kernel(
    vgrad, refine_step, mix_step, tot_2, tot_3, vgrad_out, back_out, refine_out, mix_out, back_step, sems
):
    copies = [
        pltpu.make_async_copy(source, target, sems.at[number])
        for number, (source, target) in enumerate(
            ((vgrad, vgrad_out), (refine_step, refine_out), (mix_step, mix_out), (back_step, back_out))
        )
    ]
    for copy in copies[:3]:
        copy.start()
    write_step(tot_2, tot_3, 8, back_step, mix_step.shape[0])
    copies[3].start()
    for copy in copies:
        copy.wait()


def body(volume, backbone_weight, refine_weight, mix_weight, tile_cot, tile_slot, tile_count):
    depth, rows, width = volume.shape
    channels = mix_weight.shape[0]
    edge = tile_cot.shape[4]
    owners, capacity = tile_cot.shape[2], tile_cot.shape[3]
    assert depth == edge and rows == edge and rows % 2 == 0
    lanes = 2 * channels
    pairs = width // lanes
    period = edge // 2
    slots = owners * capacity
    n_gz, n_xy = lax.axis_size("gz"), lax.axis_size("xy")
    n_x = max(n_gz // 2, 1)
    if n_xy % n_x:
        n_x = 1
    members, levels = n_gz * n_x, n_xy // n_x
    n_core = 2 if n_gz % 2 == 0 else 1
    paired = [n_core == 2 and wanted for wanted in (False, False, True, True)]
    joined = [n_core == 2 and wanted for wanted in (True, True, False, False)]

    vol = volume.reshape(depth, rows, pairs, lanes).transpose(0, 2, 1, 3)
    cot = tile_cot.reshape(slots, edge, edge, period, lanes).transpose(0, 1, 3, 2, 4)
    slot = tile_slot.reshape(owners, capacity).T
    count = tile_count.reshape(owners, owners)

    chunks, counts = [], []
    for number, tiles in enumerate((8, 7, 8, 6)):
        counts.append(members // 2 if paired[number] else members)
        chunks.append(-(-tiles * channels // (members * 16)) * 16)
    framed = pltpu.VMEM((depth + 2, rows + 2, pairs, 2 * lanes), BF16)
    band = pltpu.VMEM((48 * channels, 2 * lanes), BF16)
    wide = jax.ShapeDtypeStruct((channels, 27 * channels), F32)
    small = jax.ShapeDtypeStruct((channels, channels), F32)
    cells = depth * rows * pairs
    dma = pltpu.SemaphoreType.DMA
    step = 4 if depth % 4 == 0 else depth
    operands = (vol, cot, backbone_weight, refine_weight, mix_weight, slot, count)
    sums = [pltpu.VMEM((members * chunk, lanes), BF16) for chunk in chunks]
    pieces = []
    for number, (chunk, peers) in enumerate(zip(chunks, counts)):
        pieces += [
            sums[number],
            pltpu.VMEM((peers * chunk, lanes), BF16),
            pltpu.VMEM((peers * chunk, lanes), BF16),
            pltpu.VMEM((peers - 1, chunk, lanes), BF16),
            pltpu.VMEM((levels, chunk, lanes), BF16),
            dma((len(stages_of(paired[number], joined[number])),)),
            dma((len(stages_of(paired[number], joined[number])),)),
        ]
    vgrad, tot_2, tot_3, refine_step, mix_step = pl.pallas_call(
        functools.partial(step_kernel, n_gz, n_xy, n_x, n_core, paired, joined, period),
        out_shape=(
            jax.ShapeDtypeStruct(vol.shape, BF16),
            jax.ShapeDtypeStruct((members * chunks[2], lanes), BF16),
            jax.ShapeDtypeStruct((members * chunks[3], lanes), BF16),
            wide,
            small,
        ),
        in_specs=[HBM] * 7,
        out_specs=(VMEM,) * 5,
        scratch_shapes=[
            pltpu.VMEM(vol.shape, BF16),
            pltpu.VMEM(cot.shape, BF16),
            pltpu.VMEM(backbone_weight.shape, BF16),
            pltpu.VMEM(refine_weight.shape, BF16),
            pltpu.VMEM(mix_weight.shape, BF16),
            pltpu.SMEM(slot.shape, jnp.int32),
            pltpu.SMEM(count.shape, jnp.int32),
            pltpu.VMEM((cells, lanes), F32),
            pltpu.VMEM((depth // step, rows // 2, step, pairs, 2 * lanes), F32),
            framed, framed, framed, framed,
            band, band, band, band,
            pltpu.VMEM((cells // 2, 2 * lanes), BF16),
            pltpu.VMEM((cells // 2, 2 * lanes), BF16),
            sums[0],
            sums[1],
            dma((7,)),
            dma((8,)), dma((8,)), dma((8,)),
        ]
        + pieces,
        compiler_params=pltpu.CompilerParams(
            collective_id=0, has_side_effects=True, vmem_limit_bytes=32 * 1024 * 1024
        ),
    )(*[pltpu.with_memory_space_constraint(operand, pltpu.HBM) for operand in operands])
    vgrad, back_step, refine_step, mix_step = pl.pallas_call(
        finish_kernel,
        out_shape=(jax.ShapeDtypeStruct(vol.shape, BF16), wide, wide, small),
        in_specs=[VMEM] * 5,
        out_specs=(ANY,) * 4,
        scratch_shapes=[pltpu.VMEM(wide.shape, F32), dma((4,))],
        compiler_params=pltpu.CompilerParams(vmem_limit_bytes=8 * 1024 * 1024),
    )(vgrad, refine_step, mix_step, tot_2, tot_3)
    vgrad = vgrad.transpose(0, 2, 1, 3).reshape(depth, rows, width)
    return (vgrad, back_step, refine_step, mix_step)


def solution(mesh):
    in_specs = (
        P("gz", "xy", None),
        P(),
        P(),
        P(),
        P("gz", "xy", None, None, None, None, None),
        P("gz", "xy", None, None),
        P("gz", None, None),
    )
    out_specs = (P("gz", "xy", None), P(), P(), P())
    return jax.shard_map(body, mesh=mesh, in_specs=in_specs, out_specs=out_specs, check_vma=False)
```
